128 devices in a mesh: dp: 4 (over z_hi, core), tm: 32 (over z_lo, x, y).
Axes of the slice: x: 4, y: 4, z: 4 (z_hi: 2, z_lo: 2; z = z_hi * 2 + z_lo), core: 2. Of those that a mesh axis runs over, the one named last changes fastest.
Arguments:
- tokens: bfloat16 [4, 32, 512, 768], P('dp', 'tm'), may hold values from -60 to 60
- qkv_weight: bfloat16 [768, 2304], replicated, may hold values from -0.21875 to 0.21875
- pool_kernel: float32 [2, 27, 64], replicated, may hold values from -1.25 to 1.25
- norm_gain: float32 [2, 64], replicated, may hold values from 0.1 to 1.9
- out_weight: bfloat16 [768, 768], replicated, may hold values from -0.21875 to 0.21875
- out_cotangent: bfloat16 [4, 32, 512, 768], P('dp', 'tm'), may hold values from -6 to 6
Outputs:
- block_out: bfloat16 [4, 32, 512, 768], P('dp', 'tm')
- grad_tokens: bfloat16 [4, 32, 512, 768], P('dp', 'tm')
- grad_qkv_weight: float32 [768, 2304], P('tm')
- grad_out_weight: float32 [768, 768], P('tm')
- grad_kernel: float32 [2, 27, 64], replicated
- grad_gain: float32 [2, 64], replicated
The draws below stay inside these ranges and needn't reach their ends.
All inputs are finite; a program needn't handle non-finite values.
Results may differ from the reference program's by a relative error of at most 0.0055.
The reference program's roundings to bfloat16 on the way (of `projected`, `pooled`, `weights`, `mixed`, `d_mixed`, `scaled_grad`, `d_scores` and `d_projected`) count: a program that leaves them out, or rounds other values in their place, can miss the bound.
Values may be sent and summed in bfloat16 or wider, within the bound.
No kernel may reach another device: no remote copies, remote signals or barrier semaphores. Data moves between devices by JAX's collectives and lax.ppermute only.
A program may use at most 128 MiB of HBM per device.

```python
import math
from functools import partial
import jax
import jax.numpy as jnp
from jax import lax

D = 768
HEADS = 12
GRID_H = 32
GRID_W = 16
HEAD_DIM = 64
HW = 512
FRAMES = 32
CLIPS = 4
TOKENS = 65536


def draw_tokens(key, part):
    keys_split = jax.random.split(key, 3)
    extent = (CLIPS, FRAMES, HW, D)
    base = jax.random.normal(keys_split[0], extent, jnp.float32)
    token_scale = jnp.exp(jax.random.uniform(keys_split[1], extent[:3] + (1,), jnp.float32, 0.0, math.log(10.0)))
    channel_scale = jnp.exp(jax.random.uniform(keys_split[2], (D,), jnp.float32, math.log(0.5), math.log(2.0)))
    values = jnp.clip(0.5 * base * token_scale * channel_scale, -60.0, 60.0)
    return values.astype(jnp.bfloat16)


def shard_levels(rng, shape, cuts, smallest, high):
    loudness = 1.0
    for dim, parts in cuts:
        heights = jax.random.uniform(jax.random.fold_in(jax.random.fold_in(rng, 6), dim), (parts,), jnp.float32, smallest / len(cuts), high / len(cuts))
        loudness = loudness * jnp.repeat(jnp.exp(heights), shape[dim] // parts).reshape((-1,) + (1,) * (len(shape) - 1 - dim))
    return loudness


def bell_draw(stream_key, shape, spread, reach, cuts=(), kind=jnp.bfloat16):
    values = jax.random.normal(stream_key, shape, jnp.float32) * spread
    if len(cuts) > 0:
        values = shard_levels(stream_key, shape, cuts, -0.22, 0.18) * values
    return jnp.clip(values, min=-reach, max=reach).astype(kind)


def setup_inputs(seed: int = 0) -> dict:
    key_list = jax.random.split(jax.random.key(seed), 7)
    return {
        "tokens": draw_tokens(jax.random.fold_in(key_list[6], 71), 0),
        "qkv_weight": bell_draw(key_list[1], (D, 3 * D), D ** -0.5, 0.21875),
        "pool_kernel": bell_draw(key_list[2], (2, 27, HEAD_DIM), 27 ** -0.5, 1.25, (), jnp.float32),
        "norm_gain": jnp.clip(1.0 + 0.18 * jax.random.normal(key_list[3], (2, HEAD_DIM), jnp.float32), 0.1, 1.9),
        "out_weight": bell_draw(key_list[4], (D, D), D ** -0.5, 0.21875),
        "out_cotangent": bell_draw(key_list[5], (CLIPS, FRAMES, HW, D), 1.0, 6.0, ((0, 4), (1, 32))),
    }


EPSILON = 1e-05
pair_heads = 2

def exact_einsum(formula, first_operand, second_operand):
    return jnp.einsum(formula, first_operand.astype(jnp.float32), second_operand.astype(jnp.float32), precision=lax.Precision.HIGHEST)

def tap_table(kernel, head_count):
    tiled = jnp.tile(kernel, (1, 1, head_count))
    return jnp.transpose(tiled, (1, 0, 2)).reshape(3, 3, 3, -1)

def cut_blocks(volume):
    lead_dims = volume.ndim - 3
    extent = volume.shape
    padded = jnp.pad(volume, [(0, 0)] * lead_dims + [(1, 3), (1, 3), (0, 0)])
    pooled_h = extent[-3] // 4
    pooled_w = extent[-2] // 4
    tiled_view = padded.reshape(extent[:-3] + (pooled_h + 1, 4, pooled_w + 1, 4, extent[-1]))
    return tiled_view[..., :pooled_h, :3, :pooled_w, :3, :]

def spatial_sums(blocks, kernel_taps):
    widened = blocks.astype(jnp.float32)
    results = []
    for offset_t in range(3):
        running = None
        for offset_h in range(3):
            for offset_w in range(3):
                product_term = widened[..., offset_h, :, offset_w, :] * kernel_taps[offset_t, offset_h, offset_w]
                running = product_term if running is None else running + product_term
        results.append(running)
    return results

def spread_taps(shifted, kernel_taps, height, breadth):
    running = None
    for offset_t in range(3):
        product_term = shifted[offset_t][..., :, None, :, None, :] * kernel_taps[offset_t][:, None, :, :]
        running = product_term if running is None else running + product_term
    lead_dims = running.ndim - 5
    padded = jnp.pad(running, [(0, 0)] * lead_dims + [(0, 1)] * 4 + [(0, 0)])
    extent = padded.shape
    volume = padded.reshape(extent[:lead_dims] + (extent[lead_dims] * 4, extent[lead_dims + 2] * 4, extent[-1]))
    return volume[..., 1:height + 1, 1:breadth + 1, :]

def tap_grads(shifted, blocks, head_count):
    widened = blocks.astype(jnp.float32)
    per_offset = [jnp.einsum('cfijd,cfibjed->bed', shifted[offset_t], widened, precision=lax.Precision.HIGHEST) for offset_t in range(3)]
    stacked = jnp.stack(per_offset).reshape(27, 2, head_count, -1)
    return jnp.transpose(lax.optimization_barrier(jnp.sum(stacked, axis=2)), (1, 0, 2))

def pooled_norm(summed, gain, head_count):
    grouped_view = summed.reshape(summed.shape[:-1] + (2, head_count, -1))
    centred = grouped_view - lax.optimization_barrier(jnp.mean(grouped_view, axis=-1, keepdims=True))
    inv_std = lax.rsqrt(lax.optimization_barrier(jnp.mean(centred * centred, axis=-1, keepdims=True)) + EPSILON)
    normed = centred * inv_std
    pooled = (normed * gain[:, None, :]).reshape(summed.shape).astype(jnp.bfloat16)
    return (pooled, normed, inv_std)

def split_heads(tensor):
    extent = tensor.shape
    paired = tensor.reshape(extent[:2] + (extent[2] // pair_heads, pair_heads) + extent[3:])
    return jnp.moveaxis(paired, 2, 0)

def join_heads(tensor):
    moved = jnp.moveaxis(tensor, 0, 2)
    extent = moved.shape
    return moved.reshape(extent[:2] + (extent[2] * extent[3],) + extent[4:])

def by_pairs(function, tensors):
    results = lax.map(lambda members: function(*members), tuple((split_heads(element) for element in tensors)))
    return tuple((join_heads(element) for element in results))

def group_forward(queries, keys_part, values_part, softmax_scale):
    scores = exact_einsum('crgd,ckgd->crgk', queries, keys_part) * softmax_scale
    row_max = lax.optimization_barrier(jnp.max(scores, axis=-1))
    weights = jnp.exp(scores - row_max[..., None])
    row_total = lax.optimization_barrier(jnp.sum(weights, axis=-1))
    weighted = exact_einsum('crgk,ckgd->crgd', weights.astype(jnp.bfloat16), values_part)
    return (row_max, row_total, weighted)

def group_backward(queries, keys_part, values_part, row_max, row_total, attended, d_mixed, softmax_scale):
    scores = exact_einsum('crgd,ckgd->crgk', queries, keys_part) * softmax_scale
    weights = jnp.exp(scores - row_max[..., None])
    probability = weights / row_total[..., None]
    d_widened = d_mixed.astype(jnp.float32)
    scaled_grad = (d_widened / row_total[..., None]).astype(jnp.bfloat16)
    d_values = exact_einsum('crgk,crgd->ckgd', weights.astype(jnp.bfloat16), scaled_grad)
    d_probs = exact_einsum('crgd,ckgd->crgk', d_mixed, values_part)
    row_delta = lax.optimization_barrier(jnp.sum(d_widened * attended, axis=-1))
    d_scores = (probability * (d_probs - row_delta[..., None])).astype(jnp.bfloat16)
    d_queries = exact_einsum('crgk,ckgd->crgd', d_scores, keys_part) * softmax_scale + d_widened
    d_keys = exact_einsum('crgk,crgd->ckgd', d_scores, queries) * softmax_scale
    return (d_queries, d_keys, d_values)

def reference(tokens, qkv_weight, pool_kernel, norm_gain, out_weight, out_cotangent):
    model_width = tokens.shape[-1]
    head_size = model_width // HEADS
    softmax_scale = head_size ** (-0.5)
    kernel_taps = tap_table(pool_kernel, HEADS)

    def one_clip(members):
        clip_tokens, clip_cotangent = members
        token_rows = clip_tokens.reshape(-1, model_width)
        projected = jnp.dot(token_rows, qkv_weight, preferred_element_type=jnp.float32).astype(jnp.bfloat16)
        queries = projected[:, :model_width].reshape(1, -1, HEADS, head_size)
        volume = projected[:, model_width:].reshape(1, FRAMES, GRID_H, GRID_W, 2 * model_width)
        own_blocks = cut_blocks(volume)
        partials = spatial_sums(own_blocks, kernel_taps)
        zeros_frame = jnp.zeros_like(partials[0][:, :1])
        pooled_sum = jnp.concatenate([zeros_frame, partials[0][:, :-1]], axis=1) + partials[1] + jnp.concatenate([partials[2][:, 1:], zeros_frame], axis=1)
        pooled, normed, inv_std = pooled_norm(pooled_sum, norm_gain, HEADS)
        pooled = pooled.reshape(1, -1, 2 * model_width)
        keys_all = pooled[..., :model_width].reshape(1, -1, HEADS, head_size)
        values_all = pooled[..., model_width:].reshape(1, -1, HEADS, head_size)
        row_max, row_total, weighted = by_pairs(partial(group_forward, softmax_scale=softmax_scale), (queries, keys_all, values_all))
        attended = weighted / row_total[..., None]
        mixed = (attended + queries.astype(jnp.float32)).astype(jnp.bfloat16)
        mixed_rows = mixed.reshape(-1, model_width)
        block_out = jnp.dot(mixed_rows, out_weight, preferred_element_type=jnp.float32).astype(jnp.bfloat16)
        cotangent_rows = clip_cotangent.reshape(-1, model_width)
        d_mixed = jnp.dot(cotangent_rows, out_weight.T, preferred_element_type=jnp.float32).astype(jnp.bfloat16)
        d_mixed = d_mixed.reshape(1, -1, HEADS, head_size)
        out_local = jnp.dot(mixed_rows.T, cotangent_rows, preferred_element_type=jnp.float32)
        d_queries, d_keys, d_values = by_pairs(partial(group_backward, softmax_scale=softmax_scale), (queries, keys_all, values_all, row_max, row_total, attended, d_mixed))
        d_pooled = jnp.concatenate([d_keys.reshape(1, -1, model_width), d_values.reshape(1, -1, model_width)], axis=-1)
        d_grouped = d_pooled.reshape(normed.shape)
        sum_axes = tuple(range(normed.ndim - 3)) + (normed.ndim - 2,)
        gain_local = lax.optimization_barrier(jnp.sum(d_grouped * normed, axis=sum_axes))
        d_normed = d_grouped * norm_gain[:, None, :]
        d_summed = inv_std * (d_normed - lax.optimization_barrier(jnp.mean(d_normed, axis=-1, keepdims=True)) - normed * lax.optimization_barrier(jnp.mean(d_normed * normed, axis=-1, keepdims=True)))
        d_summed = d_summed.reshape(pooled_sum.shape)
        rims = jnp.pad(d_summed, ((0, 0), (1, 1), (0, 0), (0, 0), (0, 0)))
        shifted = [rims[:, 2:], rims[:, 1:FRAMES + 1], rims[:, :FRAMES]]
        d_volume = spread_taps(shifted, kernel_taps, GRID_H, GRID_W)
        kernel_local = tap_grads(shifted, own_blocks, HEADS)
        d_projected = jnp.concatenate([d_queries.reshape(-1, model_width), d_volume.reshape(-1, 2 * model_width)], axis=-1).astype(jnp.bfloat16)
        grad_rows = jnp.dot(d_projected, qkv_weight.T, preferred_element_type=jnp.float32).astype(jnp.bfloat16)
        qkv_local = jnp.dot(token_rows.T, d_projected, preferred_element_type=jnp.float32)
        return (block_out.reshape(clip_tokens.shape), grad_rows.reshape(clip_tokens.shape), qkv_local, out_local, kernel_local, gain_local)
    results = lax.map(one_clip, (tokens, out_cotangent))
    norm_scale = float(TOKENS) ** (-0.5)
    return (results[0], results[1], lax.optimization_barrier(jnp.sum(results[2], axis=0)) * norm_scale, lax.optimization_barrier(jnp.sum(results[3], axis=0)) * norm_scale, lax.optimization_barrier(jnp.sum(results[4], axis=0)) * norm_scale, lax.optimization_barrier(jnp.sum(results[5], axis=0)) * norm_scale)
```

```python
import jax
import jax.numpy as jnp
from jax import lax
from jax.experimental import pallas as pl
from jax.experimental.pallas import tpu as pltpu
from jax.sharding import Mesh
from jax.sharding import PartitionSpec as P

HEADS = 12
GROUPS = 4
GROUP_HEADS = 3
HEAD = 64
WIDTH = 768
SPAN = GROUP_HEADS * HEAD
HW = 512
TAPS = 288
POS = 32
EPSILON = 1e-05
TM = ("tm_0", "tm_1", "tm_2")
DP = ("dp_0", "dp_1")
BF = jnp.bfloat16
F32 = jnp.float32


def dot(a, b, ca, cb):
    return lax.dot_general(a, b, (((ca,), (cb,)), ((), ())), preferred_element_type=F32)


def params(*semantics):
    return pltpu.CompilerParams(
        dimension_semantics=semantics or None, vmem_limit_bytes=56 * 1024 * 1024
    )


def tap_token(row):
    tap = row >> 5
    i = (row & 31) >> 2
    u = row & 3
    b = jnp.where(tap >= 3, 1, 0) + jnp.where(tap >= 6, 1, 0)
    e = tap - 3 * b
    y = 4 * i + b - 1
    x = 4 * u + e - 1
    return jnp.where((y >= 0) & (x >= 0), y * 16 + x, -1)


def gather_matrix():
    row = lax.broadcasted_iota(jnp.int32, (TAPS, 1), 0)
    token = lax.broadcasted_iota(jnp.int32, (TAPS, HW), 1)
    return jnp.where(token == tap_token(row), 1.0, 0.0).astype(BF)


def scatter_matrix():
    row = lax.broadcasted_iota(jnp.int32, (1, TAPS), 1)
    token = lax.broadcasted_iota(jnp.int32, (HW, TAPS), 0)
    return jnp.where(token == tap_token(row), 1.0, 0.0).astype(BF)


def over_heads(row):
    pair = jnp.concatenate([row, row], axis=-1)
    return jnp.concatenate([pair] * (HEADS // 2), axis=-1)


def head_mean(x):
    rows = x.shape[0]
    chunks = x.shape[1] // 128
    tall = jnp.concatenate([x[:, 128 * k : 128 * k + 128] for k in range(chunks)], axis=0)
    i = lax.broadcasted_iota(jnp.int32, (128, 128), 0) >> 6
    j = lax.broadcasted_iota(jnp.int32, (128, 128), 1) >> 6
    block = jnp.where(i == j, 1.0 / 64.0, 0.0).astype(F32)
    mean = jnp.dot(tall, block, preferred_element_type=F32, precision=lax.Precision.HIGHEST)
    return jnp.concatenate([mean[rows * k : rows * k + rows] for k in range(chunks)], axis=1)


def tap_sums_kernel(tok_ref, w_ref, pk_ref, taps_ref, tt_ref, p0_ref, p1_ref, p2_ref):
    @pl.when(pl.program_id(0) == 0)
    def _():
        tt_ref[...] = dot(gather_matrix(), tok_ref[...], 1, 0).astype(BF)

    taps = dot(tt_ref[...], w_ref[...], 1, 0).astype(BF)
    taps_ref[...] = taps
    wide = taps.astype(F32)
    kernel = over_heads(pk_ref[0])
    for a, p_ref in enumerate((p0_ref, p1_ref, p2_ref)):
        total = None
        for be in range(9):
            term = wide[32 * be : 32 * be + 32] * kernel[9 * a + be : 9 * a + be + 1]
            total = term if total is None else total + term
        p_ref[...] = total


def tap_sums(tokens, qkv_weight, pool_kernel):
    part = jax.ShapeDtypeStruct((POS, 2 * WIDTH), F32)
    part_spec = pl.BlockSpec((POS, WIDTH), lambda s: (0, s))
    return pl.pallas_call(
        tap_sums_kernel,
        grid=(2,),
        in_specs=[
            pl.BlockSpec((HW, WIDTH), lambda s: (0, 0)),
            pl.BlockSpec((WIDTH, WIDTH), lambda s: (0, s + 1)),
            pl.BlockSpec((1, 27, HEAD), lambda s: (s, 0, 0)),
        ],
        out_specs=[
            pl.BlockSpec((TAPS, WIDTH), lambda s: (0, s)),
            pl.BlockSpec((TAPS, WIDTH), lambda s: (0, 0)),
            part_spec,
            part_spec,
            part_spec,
        ],
        out_shape=[
            jax.ShapeDtypeStruct((TAPS, 2 * WIDTH), BF),
            jax.ShapeDtypeStruct((TAPS, WIDTH), BF),
            part,
            part,
            part,
        ],
        compiler_params=params("arbitrary"),
        name="tap_sums",
    )(tokens, qkv_weight, pool_kernel)


def query_kernel(tok_ref, w_ref, cot_ref, ow_ref, qd_ref):
    q = dot(tok_ref[...], w_ref[...], 1, 0).astype(BF)
    dm = dot(cot_ref[...], ow_ref[...], 1, 1).astype(BF)
    for g in range(GROUPS):
        lanes = slice(SPAN * g, SPAN * g + SPAN)
        qd_ref[g] = jnp.concatenate([q[:, lanes], dm[:, lanes]], axis=-1)


def query_side(tokens, qkv_weight, cotangent, out_weight):
    full = pl.BlockSpec((HW, WIDTH), lambda i: (0, 0))
    square = pl.BlockSpec((WIDTH, WIDTH), lambda i: (0, 0))
    return pl.pallas_call(
        query_kernel,
        grid=(1,),
        in_specs=[full, square, full, square],
        out_specs=pl.BlockSpec((GROUPS, HW, 2 * SPAN), lambda i: (0, 0, 0)),
        out_shape=jax.ShapeDtypeStruct((GROUPS, HW, 2 * SPAN), BF),
        compiler_params=params("arbitrary"),
        name="query_side",
    )(tokens, qkv_weight, cotangent, out_weight)


def gain_row(gain_ref):
    return jnp.concatenate([over_heads(gain_ref[0:1, :]), over_heads(gain_ref[1:2, :])], axis=-1)


def norm_kernel(low_ref, own_ref, up_ref, gain_ref, kv_ref, normed_ref, inv_ref):
    x = low_ref[...] + own_ref[...] + up_ref[...]
    centred = x - head_mean(x)
    inv = lax.rsqrt(head_mean(centred * centred) + EPSILON)
    normed = centred * inv
    normed_ref[...] = normed
    inv_ref[...] = inv
    pooled = normed * gain_row(gain_ref)
    for g in range(GROUPS):
        k = pooled[:, SPAN * g : SPAN * g + SPAN]
        v = pooled[:, WIDTH + SPAN * g : WIDTH + SPAN * g + SPAN]
        block = jnp.concatenate([k, v], axis=-1).astype(BF)
        for z in range(2):
            for y in range(4):
                kv_ref[z, g, y] = block


def norm_side(low, own, up, gain):
    flat = jax.ShapeDtypeStruct((POS, 2 * WIDTH), F32)
    return pl.pallas_call(
        norm_kernel,
        out_shape=[jax.ShapeDtypeStruct((2, GROUPS, 4, POS, 2 * SPAN), BF), flat, flat],
        compiler_params=params(),
        name="norm_side",
    )(low, own, up, gain)


def attention_kernel(qd_ref, kv_ref, md_ref, dkv_ref, acc_ref):
    step = pl.program_id(0)

    @pl.when(step == 0)
    def _():
        acc_ref[...] = jnp.zeros_like(acc_ref)

    mixed, d_query = [], []
    for h in range(GROUP_HEADS):
        lo = slice(HEAD * h, HEAD * h + HEAD)
        hi = slice(SPAN + HEAD * h, SPAN + HEAD * h + HEAD)
        q = qd_ref[0, :, lo]
        dm = qd_ref[0, :, hi]
        k = kv_ref[:, lo]
        v = kv_ref[:, hi]
        scores = dot(q * jnp.asarray(0.125, BF), k, 1, 1)
        weights = jnp.exp(scores - jnp.max(scores, axis=-1, keepdims=True))
        inverse = 1.0 / jnp.sum(weights, axis=-1, keepdims=True)
        rounded = weights.astype(BF)
        attended = dot(rounded, v, 1, 0) * inverse
        mixed.append((attended + q.astype(F32)).astype(BF))
        wide = dm.astype(F32)
        delta = jnp.sum(wide * attended, axis=-1, keepdims=True)
        acc_ref[hi, :] += dot((wide * inverse).astype(BF), rounded, 0, 0)
        d_scores = ((weights * inverse) * (dot(dm, v, 1, 1) - delta)).astype(BF)
        d_query.append((dot(d_scores, k, 1, 0) * 0.125 + wide).astype(BF))
        acc_ref[lo, :] += dot(q, d_scores, 0, 0) * 0.125
    md_ref[0] = jnp.concatenate(mixed + d_query, axis=-1)

    @pl.when(step == pl.num_programs(0) - 1)
    def _():
        dkv_ref[...] = jnp.transpose(acc_ref[...]).astype(BF)


def attention(qd, kv):
    frames, rows, lanes = qd.shape
    keys = kv.shape[0]
    return pl.pallas_call(
        attention_kernel,
        grid=(frames,),
        in_specs=[
            pl.BlockSpec((1, rows, lanes), lambda f: (f, 0, 0)),
            pl.BlockSpec((keys, lanes), lambda f: (0, 0)),
        ],
        out_specs=[
            pl.BlockSpec((1, rows, lanes), lambda f: (f, 0, 0)),
            pl.BlockSpec((keys, lanes), lambda f: (0, 0)),
        ],
        out_shape=[
            jax.ShapeDtypeStruct(qd.shape, BF),
            jax.ShapeDtypeStruct(kv.shape, BF),
        ],
        scratch_shapes=[pltpu.VMEM((lanes, keys), F32)],
        compiler_params=params("arbitrary"),
        name="attention",
    )(qd, kv)


def norm_back_kernel(parts_ref, normed_ref, inv_ref, gain_ref, d_ref, gsum_ref):
    keys, values = [], []
    for g in range(GROUPS):
        total = None
        for z in range(2):
            for y in range(4):
                term = parts_ref[z, g, y].astype(F32)
                total = term if total is None else total + term
        keys.append(total[:, :SPAN])
        values.append(total[:, SPAN:])
    d_pooled = jnp.concatenate(keys + values, axis=-1)
    normed = normed_ref[...]
    gsum_ref[...] = jnp.sum(d_pooled * normed, axis=0, keepdims=True)
    dn = d_pooled * gain_row(gain_ref)
    d_ref[...] = inv_ref[...] * (dn - head_mean(dn) - normed * head_mean(dn * normed))


def norm_back(parts, normed, inv, gain):
    return pl.pallas_call(
        norm_back_kernel,
        out_shape=[
            jax.ShapeDtypeStruct((POS, 2 * WIDTH), F32),
            jax.ShapeDtypeStruct((1, 2 * WIDTH), F32),
        ],
        compiler_params=params(),
        name="norm_back",
    )(parts, normed, inv, gain)


def head_sum(x):
    out = []
    for s in range(2):
        pair = x[:, WIDTH * s : WIDTH * s + 128]
        for k in range(1, HEADS // 2):
            pair = pair + x[:, WIDTH * s + 128 * k : WIDTH * s + 128 * k + 128]
        out.append(pair[:, :HEAD] + pair[:, HEAD:])
    return jnp.concatenate(out, axis=-1)


def pool_back_kernel(up_ref, own_ref, low_ref, taps_ref, tt_ref, pk_ref, gsum_ref, dv_ref, pay_ref):
    kernel = jnp.concatenate([over_heads(pk_ref[0]), over_heads(pk_ref[1])], axis=-1)
    sources = (up_ref[...], own_ref[...], low_ref[...])
    tap_rows = []
    for a in range(3):
        for be in range(9):
            tap = taps_ref[32 * be : 32 * be + 32, :].astype(F32)
            tap_rows.append(jnp.sum(sources[a] * tap, axis=0, keepdims=True))
    for be in range(9):
        total = None
        for a in range(3):
            term = sources[a] * kernel[9 * a + be : 9 * a + be + 1]
            total = term if total is None else total + term
        dv_ref[32 * be : 32 * be + 32, :] = total.astype(BF)
    small = head_sum(jnp.concatenate(tap_rows + [gsum_ref[...]], axis=0))
    first = small[0:24]
    second = jnp.concatenate([small[24:28], jnp.zeros((20, 128), F32)], axis=0)
    extra = jnp.concatenate([first, second], axis=-1).astype(BF)
    grads = dot(tt_ref[...], dv_ref[...], 0, 0)
    for f in range(32):
        pay_ref[f, :, : 2 * WIDTH] = grads[24 * f : 24 * f + 24].astype(BF)
        pay_ref[f, :, 2 * WIDTH :] = extra


def pool_back(up, own, low, taps, tap_tokens, pool_kernel, gain_sum):
    return pl.pallas_call(
        pool_back_kernel,
        out_shape=[
            jax.ShapeDtypeStruct((TAPS, 2 * WIDTH), BF),
            jax.ShapeDtypeStruct((32, 24, 2 * WIDTH + 256), BF),
        ],
        compiler_params=params(),
        name="pool_back",
    )(up, own, low, taps, tap_tokens, pool_kernel, gain_sum)


def output_kernel(md_ref, tok_ref, cot_ref, ow_ref, out_ref, dq_ref, pay_ref):
    mixed = jnp.concatenate([md_ref[g, :, :SPAN] for g in range(GROUPS)], axis=-1)
    dq = jnp.concatenate([md_ref[g, :, SPAN:] for g in range(GROUPS)], axis=-1)
    dq_ref[...] = dq
    out_ref[...] = dot(mixed, ow_ref[...], 1, 0).astype(BF)
    q_grad = dot(tok_ref[...], dq, 0, 0)
    o_grad = dot(mixed, cot_ref[...], 0, 0)
    for f in range(32):
        rows = slice(24 * f, 24 * f + 24)
        pay_ref[f, :, :WIDTH] = q_grad[rows].astype(BF)
        pay_ref[f, :, WIDTH:] = o_grad[rows].astype(BF)


def output_side(md, tokens, cotangent, out_weight):
    return pl.pallas_call(
        output_kernel,
        out_shape=[
            jax.ShapeDtypeStruct((HW, WIDTH), BF),
            jax.ShapeDtypeStruct((HW, WIDTH), BF),
            jax.ShapeDtypeStruct((32, 24, 2 * WIDTH), BF),
        ],
        compiler_params=params(),
        name="output_side",
    )(md, tokens, cotangent, out_weight)


def token_grad_kernel(dq_ref, dv_ref, w_ref, out_ref):
    spread = dot(scatter_matrix(), dv_ref[...], 1, 0).astype(BF)
    total = dot(dq_ref[...], w_ref[:, :WIDTH], 1, 1) + dot(spread, w_ref[:, WIDTH:], 1, 1)
    out_ref[...] = total.astype(BF)


def token_grad(dq, dv, qkv_weight):
    return pl.pallas_call(
        token_grad_kernel,
        out_shape=jax.ShapeDtypeStruct((HW, WIDTH), BF),
        compiler_params=params(),
        name="token_grad",
    )(dq, dv, qkv_weight)


def fold_kernel(parts_ref, out_ref):
    total = parts_ref[0].astype(F32)
    for f in range(1, 32):
        total = total + parts_ref[f].astype(F32)
    for c in range(4):
        out_ref[c] = total


def fold(parts):
    return pl.pallas_call(
        fold_kernel,
        out_shape=jax.ShapeDtypeStruct((4,) + parts.shape[1:], F32),
        compiler_params=params(),
        name="fold",
    )(parts)


def finish_kernel(scale, a_ref, b_ref, qkv_ref, out_ref, kernel_ref, gain_ref):
    a = (a_ref[0] + a_ref[1] + a_ref[2] + a_ref[3]) * scale
    b = (b_ref[0] + b_ref[1] + b_ref[2] + b_ref[3]) * scale
    qkv_ref[:, :WIDTH] = a[:, :WIDTH]
    qkv_ref[:, WIDTH:] = b[:, : 2 * WIDTH]
    out_ref[...] = a[:, WIDTH:]
    first = b[:, 2 * WIDTH : 2 * WIDTH + 128]
    second = b[:, 2 * WIDTH + 128 :]
    for s in range(2):
        lanes = slice(HEAD * s, HEAD * s + HEAD)
        kernel_ref[s, 0:24, :] = first[:, lanes]
        kernel_ref[s, 24:27, :] = second[0:3, lanes]
        gain_ref[s : s + 1, :] = second[3:4, lanes]


def finish(a, b, scale):
    return pl.pallas_call(
        lambda *refs: finish_kernel(scale, *refs),
        out_shape=[
            jax.ShapeDtypeStruct((24, 3 * WIDTH), F32),
            jax.ShapeDtypeStruct((24, WIDTH), F32),
            jax.ShapeDtypeStruct((2, 27, HEAD), F32),
            jax.ShapeDtypeStruct((2, HEAD), F32),
        ],
        compiler_params=params(),
        name="finish",
    )(a, b)


def exchange(array, axis):
    return lax.all_to_all(array, axis, split_axis=0, concat_axis=0, tiled=True)


def to_next(array):
    return lax.ppermute(array, TM, [(i, i + 1) for i in range(lax.axis_size(TM) - 1)])


def to_previous(array):
    return lax.ppermute(array, TM, [(i + 1, i) for i in range(lax.axis_size(TM) - 1)])


def shards(tokens, qkv_weight, pool_kernel, norm_gain, out_weight, out_cotangent):
    shape = tokens.shape
    token_rows = tokens.reshape(HW, WIDTH)
    cotangent_rows = out_cotangent.reshape(HW, WIDTH)
    taps, tap_tokens, part0, part1, part2 = tap_sums(token_rows, qkv_weight, pool_kernel)
    low = to_next(part0)
    up = to_previous(part2)
    qd = query_side(token_rows, qkv_weight, cotangent_rows, out_weight)
    qd = exchange(qd, "tm_1")
    kv, normed, inv = norm_side(low, part1, up, norm_gain)
    kv = exchange(kv.reshape(32, POS, 2 * SPAN), TM)
    md, dkv = attention(qd, kv.reshape(32 * POS, 2 * SPAN))
    parts = exchange(dkv.reshape(32, POS, 2 * SPAN), TM)
    md = exchange(md, "tm_1")
    d_summed, gain_sum = norm_back(
        parts.reshape(2, GROUPS, 4, POS, 2 * SPAN), normed, inv, norm_gain
    )
    d_low = to_next(d_summed)
    d_up = to_previous(d_summed)
    block_out, dq, pay_a = output_side(md, token_rows, cotangent_rows, out_weight)
    pay_a = fold(exchange(pay_a, TM))
    pay_a = exchange(pay_a, DP)
    dv, pay_b = pool_back(d_up, d_summed, d_low, taps, tap_tokens, pool_kernel, gain_sum)
    pay_b = fold(exchange(pay_b, TM))
    grad_tokens = token_grad(dq, dv, qkv_weight)
    pay_b = exchange(pay_b, DP)
    scale = float(HW * lax.axis_size(DP) * lax.axis_size(TM)) ** (-0.5)
    grads = finish(pay_a, pay_b, scale)
    return (block_out.reshape(shape), grad_tokens.reshape(shape), *grads)


def solution(mesh):
    torus = Mesh(mesh.devices.reshape(2, 2, 2, 4, 4), DP + TM)
    placed = (P(DP, TM, None, None), P(), P(), P(), P(), P(DP, TM, None, None))
    return jax.shard_map(
        shards,
        mesh=torus,
        in_specs=placed,
        out_specs=(
            P(DP, TM, None, None),
            P(DP, TM, None, None),
            P(TM, None),
            P(TM, None),
            P(),
            P(),
        ),
        check_vma=False,
    )
```

```python
import jax
import jax.numpy as jnp
from jax import lax
from jax.experimental import pallas as pl
from jax.experimental.pallas import tpu as pltpu
from jax.sharding import Mesh
from jax.sharding import PartitionSpec as P

HEADS = 12
GROUPS = 4
GROUP_HEADS = 3
HEAD = 64
WIDTH = 768
SPAN = GROUP_HEADS * HEAD
HW = 512
TAPS = 288
POS = 32
EPSILON = 1e-05
HALF_B = WIDTH + 128
TM = ("tm_0", "tm_1", "tm_2")
DP = ("dp_0", "dp_1")
BF = jnp.bfloat16
F32 = jnp.float32


def dot(a, b, ca, cb):
    return lax.dot_general(a, b, (((ca,), (cb,)), ((), ())), preferred_element_type=F32)


def params(*semantics):
    return pltpu.CompilerParams(
        dimension_semantics=semantics or None, vmem_limit_bytes=56 * 1024 * 1024
    )


def tap_token(row):
    tap = row >> 5
    i = (row & 31) >> 2
    u = row & 3
    b = jnp.where(tap >= 3, 1, 0) + jnp.where(tap >= 6, 1, 0)
    e = tap - 3 * b
    y = 4 * i + b - 1
    x = 4 * u + e - 1
    return jnp.where((y >= 0) & (x >= 0), y * 16 + x, -1)


def gather_matrix():
    row = lax.broadcasted_iota(jnp.int32, (TAPS, 1), 0)
    token = lax.broadcasted_iota(jnp.int32, (TAPS, HW), 1)
    return jnp.where(token == tap_token(row), 1.0, 0.0).astype(BF)


def scatter_matrix():
    row = lax.broadcasted_iota(jnp.int32, (1, TAPS), 1)
    token = lax.broadcasted_iota(jnp.int32, (HW, TAPS), 0)
    return jnp.where(token == tap_token(row), 1.0, 0.0).astype(BF)


def over_heads(row):
    pair = jnp.concatenate([row, row], axis=-1)
    return jnp.concatenate([pair] * (HEADS // 2), axis=-1)


def head_mean(x):
    rows = x.shape[0]
    chunks = x.shape[1] // 128
    tall = jnp.concatenate([x[:, 128 * k : 128 * k + 128] for k in range(chunks)], axis=0)
    i = lax.broadcasted_iota(jnp.int32, (128, 128), 0) >> 6
    j = lax.broadcasted_iota(jnp.int32, (128, 128), 1) >> 6
    block = jnp.where(i == j, 1.0 / 64.0, 0.0).astype(F32)
    mean = jnp.dot(tall, block, preferred_element_type=F32, precision=lax.Precision.HIGHEST)
    return jnp.concatenate([mean[rows * k : rows * k + rows] for k in range(chunks)], axis=1)


def tap_sums_kernel(tok_ref, w_ref, pk_ref, taps_ref, tt_ref, p0_ref, p1_ref, p2_ref):
    @pl.when(pl.program_id(0) == 0)
    def _():
        tt_ref[...] = dot(gather_matrix(), tok_ref[...], 1, 0).astype(BF)

    taps = dot(tt_ref[...], w_ref[...], 1, 0).astype(BF)
    taps_ref[...] = taps
    wide = taps.astype(F32)
    kernel = over_heads(pk_ref[:, pl.program_id(0), :])
    for a, p_ref in enumerate((p0_ref, p1_ref, p2_ref)):
        total = None
        for be in range(9):
            term = wide[32 * be : 32 * be + 32] * kernel[9 * a + be : 9 * a + be + 1]
            total = term if total is None else total + term
        p_ref[...] = total


def tap_sums(tokens, qkv_weight, pool_kernel):
    part = jax.ShapeDtypeStruct((POS, 2 * WIDTH), F32)
    part_spec = pl.BlockSpec((POS, WIDTH), lambda s: (0, s))
    return pl.pallas_call(
        tap_sums_kernel,
        grid=(2,),
        in_specs=[
            pl.BlockSpec((HW, WIDTH), lambda s: (0, 0)),
            pl.BlockSpec((WIDTH, WIDTH), lambda s: (0, s + 1)),
            pl.BlockSpec((27, 2, HEAD), lambda s: (0, 0, 0)),
        ],
        out_specs=[
            pl.BlockSpec((TAPS, WIDTH), lambda s: (0, s)),
            pl.BlockSpec((TAPS, WIDTH), lambda s: (0, 0)),
            part_spec,
            part_spec,
            part_spec,
        ],
        out_shape=[
            jax.ShapeDtypeStruct((TAPS, 2 * WIDTH), BF),
            jax.ShapeDtypeStruct((TAPS, WIDTH), BF),
            part,
            part,
            part,
        ],
        compiler_params=params("arbitrary"),
        name="tap_sums",
    )(tokens, qkv_weight, pool_kernel)


def query_kernel(tok_ref, w_ref, cot_ref, ow_ref, *refs):
    *out_refs, group_ref = refs
    q = dot(tok_ref[...], w_ref[...], 1, 0).astype(BF)
    dm = dot(cot_ref[...], ow_ref[...], 1, 1).astype(BF)
    for g in range(GROUPS):
        lanes = slice(SPAN * g, SPAN * g + SPAN)
        group_ref[g] = jnp.concatenate([q[:, lanes], dm[:, lanes]], axis=-1)
    mine = lax.axis_index("tm_1")
    for step, out_ref in enumerate(out_refs):
        out_ref[...] = group_ref[(mine + step) % GROUPS]


def query_side(tokens, qkv_weight, cotangent, out_weight):
    full = pl.BlockSpec((HW, WIDTH), lambda i: (0, 0))
    square = pl.BlockSpec((WIDTH, WIDTH), lambda i: (0, 0))
    return pl.pallas_call(
        query_kernel,
        grid=(1,),
        in_specs=[full, square, full, square],
        out_specs=[pl.BlockSpec((HW, 2 * SPAN), lambda i: (0, 0))] * GROUPS,
        out_shape=[jax.ShapeDtypeStruct((HW, 2 * SPAN), BF)] * GROUPS,
        scratch_shapes=[pltpu.VMEM((GROUPS, HW, 2 * SPAN), BF)],
        compiler_params=params("arbitrary"),
        name="query_side",
    )(tokens, qkv_weight, cotangent, out_weight)


def gain_row(gain_ref):
    return jnp.concatenate([over_heads(gain_ref[0:1, :]), over_heads(gain_ref[1:2, :])], axis=-1)


def norm_kernel(low_ref, own_ref, up_ref, gain_ref, kv_ref, normed_ref, inv_ref):
    x = low_ref[...] + own_ref[...] + up_ref[...]
    centred = x - head_mean(x)
    inv = lax.rsqrt(head_mean(centred * centred) + EPSILON)
    normed = centred * inv
    normed_ref[...] = normed
    inv_ref[...] = inv
    pooled = normed * gain_row(gain_ref)
    for g in range(GROUPS):
        k = pooled[:, SPAN * g : SPAN * g + SPAN]
        v = pooled[:, WIDTH + SPAN * g : WIDTH + SPAN * g + SPAN]
        block = jnp.concatenate([k, v], axis=-1).astype(BF)
        for z in range(2):
            for y in range(4):
                kv_ref[z, g, y] = block


def norm_side(low, own, up, gain):
    flat = jax.ShapeDtypeStruct((POS, 2 * WIDTH), F32)
    return pl.pallas_call(
        norm_kernel,
        out_shape=[jax.ShapeDtypeStruct((2, GROUPS, 4, POS, 2 * SPAN), BF), flat, flat],
        compiler_params=params(),
        name="norm_side",
    )(low, own, up, gain)


def attend(qd, kv_ref, acc_ref):
    mixed, d_query = [], []
    for h in range(GROUP_HEADS):
        lo = slice(HEAD * h, HEAD * h + HEAD)
        hi = slice(SPAN + HEAD * h, SPAN + HEAD * h + HEAD)
        q = qd[:, lo]
        dm = qd[:, hi]
        k = kv_ref[:, lo]
        v = kv_ref[:, hi]
        scores = dot(q * jnp.asarray(0.125, BF), k, 1, 1)
        weights = jnp.exp(scores - jnp.max(scores, axis=-1, keepdims=True))
        inverse = 1.0 / jnp.sum(weights, axis=-1, keepdims=True)
        rounded = weights.astype(BF)
        attended = dot(rounded, v, 1, 0) * inverse
        mixed.append((attended + q.astype(F32)).astype(BF))
        wide = dm.astype(F32)
        delta = jnp.sum(wide * attended, axis=-1, keepdims=True)
        acc_ref[hi, :] += dot((wide * inverse).astype(BF), rounded, 0, 0)
        d_scores = ((weights * inverse) * (dot(dm, v, 1, 1) - delta)).astype(BF)
        d_query.append((dot(d_scores, k, 1, 0) * 0.125 + wide).astype(BF))
        acc_ref[lo, :] += dot(q, d_scores, 0, 0) * 0.125
    return jnp.concatenate(mixed + d_query, axis=-1)


def others_kernel(q0_ref, q1_ref, q2_ref, kv_ref, m0_ref, m1_ref, m2_ref, acc_ref, work_ref):
    acc_ref[...] = jnp.zeros_like(acc_ref)
    for n, ref in enumerate((q0_ref, q1_ref, q2_ref)):
        work_ref[n] = ref[...]

    def step(n, carry):
        work_ref[n] = attend(work_ref[n], kv_ref, acc_ref)
        return carry

    lax.fori_loop(0, 3, step, 0)
    for n, ref in enumerate((m0_ref, m1_ref, m2_ref)):
        ref[...] = work_ref[n]


def others(qds, kv):
    block = jax.ShapeDtypeStruct(qds[0].shape, BF)
    return pl.pallas_call(
        others_kernel,
        out_shape=[block, block, block, jax.ShapeDtypeStruct((kv.shape[1], kv.shape[0]), F32)],
        scratch_shapes=[pltpu.VMEM((3,) + block.shape, BF)],
        compiler_params=params(),
        name="attend_others",
    )(*qds, kv)


def own_kernel(qd_ref, kv_ref, start_ref, md_ref, dkv_ref, acc_ref):
    acc_ref[...] = start_ref[...]
    md_ref[...] = attend(qd_ref[...], kv_ref, acc_ref)
    dkv_ref[...] = jnp.transpose(acc_ref[...]).astype(BF)


def own(qd, kv, start):
    return pl.pallas_call(
        own_kernel,
        out_shape=[jax.ShapeDtypeStruct(qd.shape, BF), jax.ShapeDtypeStruct(kv.shape, BF)],
        scratch_shapes=[pltpu.VMEM(start.shape, F32)],
        compiler_params=params(),
        name="attend_own",
    )(qd, kv, start)


def norm_back_kernel(parts_ref, normed_ref, inv_ref, gain_ref, d_ref, gsum_ref):
    keys, values = [], []
    for g in range(GROUPS):
        total = None
        for z in range(2):
            for y in range(4):
                term = parts_ref[z, g, y].astype(F32)
                total = term if total is None else total + term
        keys.append(total[:, :SPAN])
        values.append(total[:, SPAN:])
    d_pooled = jnp.concatenate(keys + values, axis=-1)
    normed = normed_ref[...]
    gsum_ref[...] = jnp.sum(d_pooled * normed, axis=0, keepdims=True)
    dn = d_pooled * gain_row(gain_ref)
    d_ref[...] = inv_ref[...] * (dn - head_mean(dn) - normed * head_mean(dn * normed))


def norm_back(parts, normed, inv, gain):
    return pl.pallas_call(
        norm_back_kernel,
        out_shape=[
            jax.ShapeDtypeStruct((POS, 2 * WIDTH), F32),
            jax.ShapeDtypeStruct((1, 2 * WIDTH), F32),
        ],
        compiler_params=params(),
        name="norm_back",
    )(parts, normed, inv, gain)


def head_sum(x):
    out = []
    for s in range(2):
        pair = x[:, WIDTH * s : WIDTH * s + 128]
        for k in range(1, HEADS // 2):
            pair = pair + x[:, WIDTH * s + 128 * k : WIDTH * s + 128 * k + 128]
        out.append(pair[:, :HEAD] + pair[:, HEAD:])
    return jnp.concatenate(out, axis=-1)


def pool_back_kernel(up_ref, own_ref, low_ref, taps_ref, tt_ref, pk_ref, gsum_ref, dv_ref, *pays):
    kernel = jnp.concatenate([over_heads(pk_ref[:, 0, :]), over_heads(pk_ref[:, 1, :])], axis=-1)
    sources = (up_ref[...], own_ref[...], low_ref[...])
    tap_rows = []
    for a in range(3):
        for be in range(9):
            tap = taps_ref[32 * be : 32 * be + 32, :].astype(F32)
            tap_rows.append(jnp.sum(sources[a] * tap, axis=0, keepdims=True))
    for be in range(9):
        total = None
        for a in range(3):
            term = sources[a] * kernel[9 * a + be : 9 * a + be + 1]
            total = term if total is None else total + term
        dv_ref[32 * be : 32 * be + 32, :] = total.astype(BF)
    small = head_sum(jnp.concatenate(tap_rows + [gsum_ref[...]], axis=0))
    first = small[0:24]
    second = jnp.concatenate([small[24:28], jnp.zeros((20, 128), F32)], axis=0)
    extra = jnp.concatenate([first, second], axis=-1).astype(BF)
    grads = dot(tt_ref[...], dv_ref[...], 0, 0)
    keep_ref, send_ref, half_ref = pays
    for f in range(32):
        rows = jnp.concatenate([grads[24 * f : 24 * f + 24].astype(BF), extra], axis=-1)
        half_ref[0, f] = rows[:, :HALF_B]
        half_ref[1, f] = rows[:, HALF_B:]
    core = lax.axis_index("dp_1")
    keep_ref[...] = half_ref[core]
    send_ref[...] = half_ref[1 - core]


def pool_back(up, own, low, taps, tap_tokens, pool_kernel, gain_sum):
    return pl.pallas_call(
        pool_back_kernel,
        out_shape=[
            jax.ShapeDtypeStruct((TAPS, 2 * WIDTH), BF),
            jax.ShapeDtypeStruct((32, 24, HALF_B), BF),
            jax.ShapeDtypeStruct((32, 24, HALF_B), BF),
        ],
        scratch_shapes=[pltpu.VMEM((2, 32, 24, HALF_B), BF)],
        compiler_params=params(),
        name="pool_back",
    )(up, own, low, taps, tap_tokens, pool_kernel, gain_sum)


def output_kernel(m0_ref, m1_ref, m2_ref, m3_ref, tok_ref, cot_ref, ow_ref, *refs):
    out_ref, dq_ref, keep_ref, send_ref, group_ref, half_ref = refs
    mine = lax.axis_index("tm_1")
    for step, ref in enumerate((m0_ref, m1_ref, m2_ref, m3_ref)):
        group_ref[(mine + step) % GROUPS] = ref[...]
    mixed = jnp.concatenate([group_ref[g, :, :SPAN] for g in range(GROUPS)], axis=-1)
    dq = jnp.concatenate([group_ref[g, :, SPAN:] for g in range(GROUPS)], axis=-1)
    dq_ref[...] = dq
    out_ref[...] = dot(mixed, ow_ref[...], 1, 0).astype(BF)
    q_grad = dot(tok_ref[...], dq, 0, 0)
    o_grad = dot(mixed, cot_ref[...], 0, 0)
    for f in range(32):
        rows = slice(24 * f, 24 * f + 24)
        half_ref[0, f] = q_grad[rows].astype(BF)
        half_ref[1, f] = o_grad[rows].astype(BF)
    core = lax.axis_index("dp_1")
    keep_ref[...] = half_ref[core]
    send_ref[...] = half_ref[1 - core]


def output_side(mds, tokens, cotangent, out_weight):
    half = jax.ShapeDtypeStruct((32, 24, WIDTH), BF)
    rows = jax.ShapeDtypeStruct((HW, WIDTH), BF)
    return pl.pallas_call(
        output_kernel,
        out_shape=[rows, rows, half, half],
        scratch_shapes=[
            pltpu.VMEM((GROUPS, HW, 2 * SPAN), BF),
            pltpu.VMEM((2, 32, 24, WIDTH), BF),
        ],
        compiler_params=params(),
        name="output_side",
    )(*mds, tokens, cotangent, out_weight)


def token_grad_kernel(dq_ref, dv_ref, w_ref, out_ref):
    spread = dot(scatter_matrix(), dv_ref[...], 1, 0).astype(BF)
    total = dot(dq_ref[...], w_ref[:, :WIDTH], 1, 1) + dot(spread, w_ref[:, WIDTH:], 1, 1)
    out_ref[...] = total.astype(BF)


def token_grad(dq, dv, qkv_weight):
    return pl.pallas_call(
        token_grad_kernel,
        out_shape=jax.ShapeDtypeStruct((HW, WIDTH), BF),
        compiler_params=params(),
        name="token_grad",
    )(dq, dv, qkv_weight)


def fold_kernel(parts_ref, out_ref):
    total = parts_ref[0].astype(F32)
    for f in range(1, 32):
        total = total + parts_ref[f].astype(F32)
    out_ref[...] = total


def fold(parts):
    return pl.pallas_call(
        fold_kernel,
        out_shape=jax.ShapeDtypeStruct(parts.shape[1:], F32),
        compiler_params=params(),
        name="fold",
    )(parts)


def finish_kernel(scale, a0, a1, a2, a3, b0, b1, b2, b3, qkv_ref, out_ref, kernel_ref, gain_ref, a_ref, b_ref):
    core = lax.axis_index("dp_1")
    a_ref[core] = (a0[...] + a2[...]) * scale
    a_ref[1 - core] = (a1[...] + a3[...]) * scale
    b_ref[core] = (b0[...] + b2[...]) * scale
    b_ref[1 - core] = (b1[...] + b3[...]) * scale
    qkv_ref[:, :WIDTH] = a_ref[0]
    qkv_ref[:, WIDTH : WIDTH + HALF_B] = b_ref[0]
    qkv_ref[:, WIDTH + HALF_B :] = b_ref[1, :, : 2 * WIDTH - HALF_B]
    out_ref[...] = a_ref[1]
    first = b_ref[1, :, HALF_B - 256 : HALF_B - 128]
    second = b_ref[1, :, HALF_B - 128 :]
    for s in range(2):
        lanes = slice(HEAD * s, HEAD * s + HEAD)
        kernel_ref[0:24, s, :] = first[:, lanes]
        kernel_ref[24:27, s, :] = second[0:3, lanes]
        gain_ref[s : s + 1, :] = second[3:4, lanes]


def finish(a, b, scale):
    return pl.pallas_call(
        lambda *refs: finish_kernel(scale, *refs),
        out_shape=[
            jax.ShapeDtypeStruct((24, 3 * WIDTH), F32),
            jax.ShapeDtypeStruct((24, WIDTH), F32),
            jax.ShapeDtypeStruct((27, 2, HEAD), F32),
            jax.ShapeDtypeStruct((2, HEAD), F32),
        ],
        scratch_shapes=[pltpu.VMEM((2, 24, WIDTH), F32), pltpu.VMEM((2, 24, HALF_B), F32)],
        compiler_params=params(),
        name="finish",
    )(*a, *b)


def exchange(array, axis):
    return lax.all_to_all(array, axis, split_axis=0, concat_axis=0, tiled=True)


def to_next(array):
    return lax.ppermute(array, TM, [(i, i + 1) for i in range(lax.axis_size(TM) - 1)])


def to_previous(array):
    return lax.ppermute(array, TM, [(i + 1, i) for i in range(lax.axis_size(TM) - 1)])


def rotate(array, steps):
    return lax.ppermute(array, "tm_1", [(i, (i + steps) % GROUPS) for i in range(GROUPS)])


def core_sum(keep, send):
    other = lax.ppermute(send, "dp_1", [(0, 1), (1, 0)])
    return (keep.astype(F32) + other.astype(F32)).astype(BF)


def copies(array):
    return [array] + [lax.ppermute(array, DP, [(i, i ^ k) for i in range(4)]) for k in (1, 2, 3)]


def block(tokens, qkv_weight, pool_kernel, norm_gain, out_weight, out_cotangent):
    shape = tokens.shape
    token_rows = tokens.reshape(HW, WIDTH)
    cotangent_rows = out_cotangent.reshape(HW, WIDTH)
    pool_kernel = jnp.transpose(pool_kernel, (1, 0, 2))
    taps, tap_tokens, part0, part1, part2 = tap_sums(token_rows, qkv_weight, pool_kernel)
    low = to_next(part0)
    up = to_previous(part2)
    qd, *qds = query_side(token_rows, qkv_weight, cotangent_rows, out_weight)
    received = [rotate(q, k) for k, q in zip((1, 2, 3), qds)]
    kv, normed, inv = norm_side(low, part1, up, norm_gain)
    kv = exchange(kv.reshape(32, POS, 2 * SPAN), TM)
    kv = kv.reshape(32 * POS, 2 * SPAN)
    *mds, start = others(received, kv)
    mds = [rotate(m, -k) for k, m in zip((1, 2, 3), mds)]
    md, dkv = own(qd, kv, start)
    parts = exchange(dkv.reshape(32, POS, 2 * SPAN), TM)
    parts = parts.reshape(2, GROUPS, 4, POS, 2 * SPAN)
    d_summed, gain_sum = norm_back(parts, normed, inv, norm_gain)
    d_low = to_next(d_summed)
    d_up = to_previous(d_summed)
    block_out, dq, *pay_a = output_side([md] + mds, token_rows, cotangent_rows, out_weight)
    pay_a = core_sum(*pay_a)
    pay_a = exchange(pay_a, TM)
    pay_a = copies(fold(pay_a))
    dv, *pay_b = pool_back(d_up, d_summed, d_low, taps, tap_tokens, pool_kernel, gain_sum)
    pay_b = core_sum(*pay_b)
    pay_b = exchange(pay_b, TM)
    pay_b = copies(fold(pay_b))
    grad_tokens = token_grad(dq, dv, qkv_weight)
    scale = float(HW * lax.axis_size(DP) * lax.axis_size(TM)) ** (-0.5)
    qkv_grad, out_grad, kernel_grad, gain_grad = finish(pay_a, pay_b, scale)
    return (
        block_out.reshape(shape),
        grad_tokens.reshape(shape),
        qkv_grad,
        out_grad,
        jnp.transpose(kernel_grad, (1, 0, 2)),
        gain_grad,
    )


def solution(mesh):
    torus = Mesh(mesh.devices.reshape(2, 2, 2, 4, 4), DP + TM)
    placed = (P(DP, TM, None, None), P(), P(), P(), P(), P(DP, TM, None, None))
    return jax.shard_map(
        block,
        mesh=torus,
        in_specs=placed,
        out_specs=(
            P(DP, TM, None, None),
            P(DP, TM, None, None),
            P(TM, None),
            P(TM, None),
            P(),
            P(),
        ),
        check_vma=False,
    )
```

```python
import jax
import jax.numpy as jnp
from jax import lax
from jax.experimental import pallas as pl
from jax.experimental.pallas import tpu as pltpu
from jax.sharding import Mesh
from jax.sharding import PartitionSpec as P

HEADS = 12
GROUPS = 4
GROUP_HEADS = 3
HEAD = 64
WIDTH = 768
SPAN = GROUP_HEADS * HEAD
HW = 512
TAPS = 288
POS = 32
EPSILON = 1e-05
PAY_B = WIDTH + 256
TM = ("tm_0", "tm_1", "tm_2")
DP = ("dp_0", "dp_1")
BF = jnp.bfloat16
F32 = jnp.float32


def dot(a, b, ca, cb):
    return lax.dot_general(a, b, (((ca,), (cb,)), ((), ())), preferred_element_type=F32)


def params(*semantics):
    return pltpu.CompilerParams(
        dimension_semantics=semantics or None, vmem_limit_bytes=56 * 1024 * 1024
    )


def tap_token(row):
    tap = row >> 5
    i = (row & 31) >> 2
    u = row & 3
    b = jnp.where(tap >= 3, 1, 0) + jnp.where(tap >= 6, 1, 0)
    e = tap - 3 * b
    y = 4 * i + b - 1
    x = 4 * u + e - 1
    return jnp.where((y >= 0) & (x >= 0), y * 16 + x, -1)


def gather_matrix():
    row = lax.broadcasted_iota(jnp.int32, (TAPS, 1), 0)
    token = lax.broadcasted_iota(jnp.int32, (TAPS, HW), 1)
    return jnp.where(token == tap_token(row), 1.0, 0.0).astype(BF)


def scatter_matrix():
    row = lax.broadcasted_iota(jnp.int32, (1, TAPS), 1)
    token = lax.broadcasted_iota(jnp.int32, (HW, TAPS), 0)
    return jnp.where(token == tap_token(row), 1.0, 0.0).astype(BF)


def over_heads(row):
    pair = jnp.concatenate([row, row], axis=-1)
    return jnp.concatenate([pair] * (HEADS // 2), axis=-1)


def head_mean(x):
    rows = x.shape[0]
    chunks = x.shape[1] // 128
    tall = jnp.concatenate([x[:, 128 * k : 128 * k + 128] for k in range(chunks)], axis=0)
    i = lax.broadcasted_iota(jnp.int32, (128, 128), 0) >> 6
    j = lax.broadcasted_iota(jnp.int32, (128, 128), 1) >> 6
    block = jnp.where(i == j, 1.0 / 64.0, 0.0).astype(F32)
    mean = jnp.dot(tall, block, preferred_element_type=F32, precision=lax.Precision.HIGHEST)
    return jnp.concatenate([mean[rows * k : rows * k + rows] for k in range(chunks)], axis=1)


def tap_sums_kernel(tok_ref, w_ref, pk_ref, taps_ref, tt_ref, p0_ref, p1_ref, p2_ref):
    @pl.when(pl.program_id(0) == 0)
    def _():
        tt_ref[...] = dot(gather_matrix(), tok_ref[...], 1, 0).astype(BF)

    taps = dot(tt_ref[...], w_ref[...], 1, 0).astype(BF)
    taps_ref[...] = taps
    wide = taps.astype(F32)
    kernel = over_heads(pk_ref[:, pl.program_id(0), :])
    for a, p_ref in enumerate((p0_ref, p1_ref, p2_ref)):
        total = None
        for be in range(9):
            term = wide[32 * be : 32 * be + 32] * kernel[9 * a + be : 9 * a + be + 1]
            total = term if total is None else total + term
        p_ref[...] = total


def tap_sums(tokens, qkv_weight, pool_kernel):
    part = jax.ShapeDtypeStruct((POS, 2 * WIDTH), F32)
    part_spec = pl.BlockSpec((POS, WIDTH), lambda s: (0, s))
    return pl.pallas_call(
        tap_sums_kernel,
        grid=(2,),
        in_specs=[
            pl.BlockSpec((HW, WIDTH), lambda s: (0, 0)),
            pl.BlockSpec((WIDTH, WIDTH), lambda s: (0, s + 1)),
            pl.BlockSpec((27, 2, HEAD), lambda s: (0, 0, 0)),
        ],
        out_specs=[
            pl.BlockSpec((TAPS, WIDTH), lambda s: (0, s)),
            pl.BlockSpec((TAPS, WIDTH), lambda s: (0, 0)),
            part_spec,
            part_spec,
            part_spec,
        ],
        out_shape=[
            jax.ShapeDtypeStruct((TAPS, 2 * WIDTH), BF),
            jax.ShapeDtypeStruct((TAPS, WIDTH), BF),
            part,
            part,
            part,
        ],
        compiler_params=params("arbitrary"),
        name="tap_sums",
    )(tokens, qkv_weight, pool_kernel)


def query_kernel(tok_ref, w_ref, cot_ref, ow_ref, *refs):
    *out_refs, group_ref = refs
    q = dot(tok_ref[...], w_ref[...], 1, 0).astype(BF)
    dm = dot(cot_ref[...], ow_ref[...], 1, 1).astype(BF)
    for g in range(GROUPS):
        lanes = slice(SPAN * g, SPAN * g + SPAN)
        group_ref[g] = jnp.concatenate([q[:, lanes], dm[:, lanes]], axis=-1)
    mine = lax.axis_index("tm_1")
    for step, out_ref in enumerate(out_refs):
        out_ref[...] = group_ref[(mine + step) % GROUPS]


def query_side(tokens, qkv_weight, cotangent, out_weight):
    full = pl.BlockSpec((HW, WIDTH), lambda i: (0, 0))
    square = pl.BlockSpec((WIDTH, WIDTH), lambda i: (0, 0))
    return pl.pallas_call(
        query_kernel,
        grid=(1,),
        in_specs=[full, square, full, square],
        out_specs=[pl.BlockSpec((HW, 2 * SPAN), lambda i: (0, 0))] * GROUPS,
        out_shape=[jax.ShapeDtypeStruct((HW, 2 * SPAN), BF)] * GROUPS,
        scratch_shapes=[pltpu.VMEM((GROUPS, HW, 2 * SPAN), BF)],
        compiler_params=params("arbitrary"),
        name="query_side",
    )(tokens, qkv_weight, cotangent, out_weight)


def gain_row(gain_ref):
    return jnp.concatenate([over_heads(gain_ref[0:1, :]), over_heads(gain_ref[1:2, :])], axis=-1)


def norm_kernel(low_ref, own_ref, up_ref, gain_ref, kv_ref, normed_ref, inv_ref):
    x = low_ref[...] + own_ref[...] + up_ref[...]
    centred = x - head_mean(x)
    inv = lax.rsqrt(head_mean(centred * centred) + EPSILON)
    normed = centred * inv
    normed_ref[...] = normed
    inv_ref[...] = inv
    pooled = normed * gain_row(gain_ref)
    for g in range(GROUPS):
        k = pooled[:, SPAN * g : SPAN * g + SPAN]
        v = pooled[:, WIDTH + SPAN * g : WIDTH + SPAN * g + SPAN]
        block = jnp.concatenate([k, v], axis=-1).astype(BF)
        for z in range(2):
            for y in range(4):
                kv_ref[z, g, y] = block


def norm_side(low, own, up, gain):
    flat = jax.ShapeDtypeStruct((POS, 2 * WIDTH), F32)
    return pl.pallas_call(
        norm_kernel,
        out_shape=[jax.ShapeDtypeStruct((2, GROUPS, 4, POS, 2 * SPAN), BF), flat, flat],
        compiler_params=params(),
        name="norm_side",
    )(low, own, up, gain)


def attend(qd, kv_ref, acc_ref):
    n = GROUP_HEADS
    lo = [slice(HEAD * h, HEAD * h + HEAD) for h in range(n)]
    hi = [slice(SPAN + HEAD * h, SPAN + HEAD * h + HEAD) for h in range(n)]
    q = [qd[:, lo[h]] for h in range(n)]
    dm = [qd[:, hi[h]] for h in range(n)]
    k = [kv_ref[:, lo[h]] for h in range(n)]
    v = [kv_ref[:, hi[h]] for h in range(n)]
    s, w, inv, rounded, dp, ds, delta = ({} for _ in range(7))
    mixed, dq = {}, {}
    def score(h):
        s[h] = dot(q[h] * jnp.asarray(0.125, BF), k[h], 1, 1)
    def grad_probs(h):
        dp[h] = dot(dm[h], v[h], 1, 1)
    def soften(h):
        w[h] = jnp.exp(s[h] - jnp.max(s[h], axis=-1, keepdims=True))
        inv[h] = 1.0 / jnp.sum(w[h], axis=-1, keepdims=True)
        rounded[h] = w[h].astype(BF)
    def mix(h):
        attended = lax.transpose(dot(v[h], rounded[h], 0, 1), (1, 0)) * inv[h]
        mixed[h] = (attended + q[h].astype(F32)).astype(BF)
        wide = dm[h].astype(F32)
        delta[h] = jnp.sum(wide * attended, axis=-1, keepdims=True)
    def grad_values(h):
        acc_ref[hi[h], :] += dot((dm[h].astype(F32) * inv[h]).astype(BF), rounded[h], 0, 0)
    def grad_scores(h):
        ds[h] = ((w[h] * inv[h]) * (dp[h] - delta[h])).astype(BF)
    def grad_rest(h):
        dq[h] = (dot(ds[h], k[h], 1, 0) * 0.125 + dm[h].astype(F32)).astype(BF)
        acc_ref[lo[h], :] += dot(q[h], ds[h], 0, 0) * 0.125
    order = (
        (score, 0), (soften, 0), (score, 1), (grad_probs, 0), (mix, 0), (soften, 1),
        (grad_values, 0), (grad_scores, 0), (mix, 1), (grad_probs, 1), (score, 2), (grad_rest, 0),
        (soften, 2), (grad_scores, 1), (grad_values, 1), (mix, 2), (grad_probs, 2), (grad_rest, 1),
        (grad_scores, 2), (grad_values, 2), (grad_rest, 2),
    )
    for function, h in order:
        function(h)
    return jnp.concatenate([mixed[h] for h in range(n)] + [dq[h] for h in range(n)], axis=-1)


def others_kernel(q0_ref, q1_ref, q2_ref, kv_ref, m0_ref, m1_ref, m2_ref, acc_ref, work_ref):
    acc_ref[...] = jnp.zeros_like(acc_ref)
    for n, ref in enumerate((q0_ref, q1_ref, q2_ref)):
        work_ref[n] = ref[...]

    def step(n, carry):
        work_ref[n] = attend(work_ref[n], kv_ref, acc_ref)
        return carry

    lax.fori_loop(0, 3, step, 0)
    for n, ref in enumerate((m0_ref, m1_ref, m2_ref)):
        ref[...] = work_ref[n]


def others(qds, kv):
    block = jax.ShapeDtypeStruct(qds[0].shape, BF)
    return pl.pallas_call(
        others_kernel,
        out_shape=[block, block, block, jax.ShapeDtypeStruct((kv.shape[1], kv.shape[0]), F32)],
        scratch_shapes=[pltpu.VMEM((3,) + block.shape, BF)],
        compiler_params=params(),
        name="attend_others",
    )(*qds, kv)


def own_kernel(qd_ref, kv_ref, start_ref, md_ref, dkv_ref, acc_ref):
    acc_ref[...] = start_ref[...]
    md_ref[...] = attend(qd_ref[...], kv_ref, acc_ref)
    dkv_ref[...] = jnp.transpose(acc_ref[...]).astype(BF)


def own(qd, kv, start):
    return pl.pallas_call(
        own_kernel,
        out_shape=[jax.ShapeDtypeStruct(qd.shape, BF), jax.ShapeDtypeStruct(kv.shape, BF)],
        scratch_shapes=[pltpu.VMEM(start.shape, F32)],
        compiler_params=params(),
        name="attend_own",
    )(qd, kv, start)


def norm_back_kernel(parts_ref, normed_ref, inv_ref, gain_ref, d_ref, gsum_ref):
    keys, values = [], []
    for g in range(GROUPS):
        total = None
        for z in range(2):
            for y in range(4):
                term = parts_ref[z, g, y].astype(F32)
                total = term if total is None else total + term
        keys.append(total[:, :SPAN])
        values.append(total[:, SPAN:])
    d_pooled = jnp.concatenate(keys + values, axis=-1)
    normed = normed_ref[...]
    gsum_ref[...] = jnp.sum(d_pooled * normed, axis=0, keepdims=True)
    dn = d_pooled * gain_row(gain_ref)
    d_ref[...] = inv_ref[...] * (dn - head_mean(dn) - normed * head_mean(dn * normed))


def norm_back(parts, normed, inv, gain):
    return pl.pallas_call(
        norm_back_kernel,
        out_shape=[
            jax.ShapeDtypeStruct((POS, 2 * WIDTH), F32),
            jax.ShapeDtypeStruct((1, 2 * WIDTH), F32),
        ],
        compiler_params=params(),
        name="norm_back",
    )(parts, normed, inv, gain)


def head_sum(x):
    out = []
    for s in range(2):
        pair = x[:, WIDTH * s : WIDTH * s + 128]
        for k in range(1, HEADS // 2):
            pair = pair + x[:, WIDTH * s + 128 * k : WIDTH * s + 128 * k + 128]
        out.append(pair[:, :HEAD] + pair[:, HEAD:])
    return jnp.concatenate(out, axis=-1)


def dest_rows(f):
    return slice(24 * f, 24 * f + 24)


def pool_back_kernel(up_ref, own_ref, low_ref, taps_ref, tt_ref, pk_ref, gsum_ref, *out_refs):
    dv_ref, send_ref, small_ref = out_refs
    sources = (up_ref[...], own_ref[...], low_ref[...])
    for s in range(2):
        lanes = slice(WIDTH * s, WIDTH * s + WIDTH)
        kernel = over_heads(pk_ref[:, s, :])
        for be in range(9):
            total = None
            for a in range(3):
                term = sources[a][:, lanes] * kernel[9 * a + be : 9 * a + be + 1]
                total = term if total is None else total + term
            dv_ref[s, 32 * be : 32 * be + 32, :] = total.astype(BF)
    grads = dot(tt_ref[...], dv_ref[1 - lax.axis_index("dp_1")], 0, 0)
    for f in range(32):
        send_ref[f] = grads[dest_rows(f)].astype(BF)
    tap_rows = []
    for a in range(3):
        for be in range(9):
            tap = taps_ref[32 * be : 32 * be + 32, :].astype(F32)
            tap_rows.append(jnp.sum(sources[a] * tap, axis=0, keepdims=True))
    small = head_sum(jnp.concatenate(tap_rows + [gsum_ref[...]], axis=0))
    second = jnp.concatenate([small[24:28], jnp.zeros((20, 128), F32)], axis=0)
    small_ref[...] = jnp.concatenate([small[0:24], second], axis=-1)


def pool_back(up, own, low, taps, tap_tokens, pool_kernel, gain_sum):
    return pl.pallas_call(
        pool_back_kernel,
        out_shape=[
            jax.ShapeDtypeStruct((2, TAPS, WIDTH), BF),
            jax.ShapeDtypeStruct((32, 24, WIDTH), BF),
            jax.ShapeDtypeStruct((24, 256), F32),
        ],
        compiler_params=params(),
        name="pool_back",
    )(up, own, low, taps, tap_tokens, pool_kernel, gain_sum)


def pay_b_kernel(tt_ref, dv_ref, other_ref, small_ref, other_small_ref, out_ref):
    core = lax.axis_index("dp_1")
    grads = dot(tt_ref[...], dv_ref[core], 0, 0)
    small = small_ref[...] + other_small_ref[...]
    high = small.astype(BF).astype(F32)
    extra = jnp.where(core == 0, high, small - high).astype(BF)
    for f in range(32):
        total = grads[dest_rows(f)] + other_ref[f].astype(F32)
        out_ref[f, :, :WIDTH] = total.astype(BF)
        out_ref[f, :, WIDTH:] = extra


def pay_b_rows(tap_tokens, dv, other, small, other_small):
    return pl.pallas_call(
        pay_b_kernel,
        out_shape=jax.ShapeDtypeStruct((32, 24, PAY_B), BF),
        compiler_params=params(),
        name="pay_b_rows",
    )(tap_tokens, dv, other, small, other_small)


def output_kernel(m0_ref, m1_ref, m2_ref, m3_ref, tok_ref, cot_ref, ow_ref, *refs):
    out_ref, dq_ref, keep_ref, send_ref, group_ref, half_ref = refs
    mine = lax.axis_index("tm_1")
    for step, ref in enumerate((m0_ref, m1_ref, m2_ref, m3_ref)):
        group_ref[(mine + step) % GROUPS] = ref[...]
    mixed = jnp.concatenate([group_ref[g, :, :SPAN] for g in range(GROUPS)], axis=-1)
    dq = jnp.concatenate([group_ref[g, :, SPAN:] for g in range(GROUPS)], axis=-1)
    dq_ref[...] = dq
    out_ref[...] = dot(mixed, ow_ref[...], 1, 0).astype(BF)
    q_grad = dot(tok_ref[...], dq, 0, 0)
    o_grad = dot(mixed, cot_ref[...], 0, 0)
    for f in range(32):
        rows = slice(24 * f, 24 * f + 24)
        half_ref[0, f] = q_grad[rows].astype(BF)
        half_ref[1, f] = o_grad[rows].astype(BF)
    core = lax.axis_index("dp_1")
    keep_ref[...] = half_ref[core]
    send_ref[...] = half_ref[1 - core]


def output_side(mds, tokens, cotangent, out_weight):
    half = jax.ShapeDtypeStruct((32, 24, WIDTH), BF)
    rows = jax.ShapeDtypeStruct((HW, WIDTH), BF)
    return pl.pallas_call(
        output_kernel,
        out_shape=[rows, rows, half, half],
        scratch_shapes=[
            pltpu.VMEM((GROUPS, HW, 2 * SPAN), BF),
            pltpu.VMEM((2, 32, 24, WIDTH), BF),
        ],
        compiler_params=params(),
        name="output_side",
    )(*mds, tokens, cotangent, out_weight)


def token_grad_kernel(dq_ref, dv_ref, w_ref, out_ref):
    scatter = scatter_matrix()
    total = dot(dq_ref[...], w_ref[:, :WIDTH], 1, 1)
    for s in range(2):
        spread = dot(scatter, dv_ref[s], 1, 0).astype(BF)
        total += dot(spread, w_ref[:, WIDTH * (s + 1) : WIDTH * (s + 2)], 1, 1)
    out_ref[...] = total.astype(BF)


def token_grad(dq, dv, qkv_weight):
    return pl.pallas_call(
        token_grad_kernel,
        out_shape=jax.ShapeDtypeStruct((HW, WIDTH), BF),
        compiler_params=params(),
        name="token_grad",
    )(dq, dv, qkv_weight)


def fold_kernel(parts_ref, out_ref):
    total = parts_ref[0].astype(F32)
    for f in range(1, 32):
        total = total + parts_ref[f].astype(F32)
    out_ref[...] = total


def fold(parts):
    return pl.pallas_call(
        fold_kernel,
        out_shape=jax.ShapeDtypeStruct(parts.shape[1:], F32),
        compiler_params=params(),
        name="fold",
    )(parts)


def finish_kernel(scale, a0, a1, a2, a3, b0, b1, b2, b3, qkv_ref, out_ref, kernel_ref, gain_ref, a_ref, b_ref):
    core = lax.axis_index("dp_1")
    a_ref[core] = (a0[...] + a2[...]) * scale
    a_ref[1 - core] = (a1[...] + a3[...]) * scale
    b_ref[core] = (b0[...] + b2[...]) * scale
    b_ref[1 - core] = (b1[...] + b3[...]) * scale
    qkv_ref[:, :WIDTH] = a_ref[0]
    qkv_ref[:, WIDTH : 2 * WIDTH] = b_ref[0, :, :WIDTH]
    qkv_ref[:, 2 * WIDTH :] = b_ref[1, :, :WIDTH]
    out_ref[...] = a_ref[1]
    small = b_ref[0, :, WIDTH:] + b_ref[1, :, WIDTH:]
    first = small[:, :128]
    second = small[:, 128:]
    for s in range(2):
        lanes = slice(HEAD * s, HEAD * s + HEAD)
        kernel_ref[0:24, s, :] = first[:, lanes]
        kernel_ref[24:27, s, :] = second[0:3, lanes]
        gain_ref[s : s + 1, :] = second[3:4, lanes]


def finish(a, b, scale):
    return pl.pallas_call(
        lambda *refs: finish_kernel(scale, *refs),
        out_shape=[
            jax.ShapeDtypeStruct((24, 3 * WIDTH), F32),
            jax.ShapeDtypeStruct((24, WIDTH), F32),
            jax.ShapeDtypeStruct((27, 2, HEAD), F32),
            jax.ShapeDtypeStruct((2, HEAD), F32),
        ],
        scratch_shapes=[pltpu.VMEM((2, 24, WIDTH), F32), pltpu.VMEM((2, 24, PAY_B), F32)],
        compiler_params=params(),
        name="finish",
    )(*a, *b)


def exchange(array, axis):
    return lax.all_to_all(array, axis, split_axis=0, concat_axis=0, tiled=True)


def to_next(array):
    return lax.ppermute(array, TM, [(i, i + 1) for i in range(lax.axis_size(TM) - 1)])


def to_previous(array):
    return lax.ppermute(array, TM, [(i + 1, i) for i in range(lax.axis_size(TM) - 1)])


def rotate(array, steps):
    return lax.ppermute(array, "tm_1", [(i, (i + steps) % GROUPS) for i in range(GROUPS)])


def swap_cores(array):
    return lax.ppermute(array, "dp_1", [(0, 1), (1, 0)])


def core_sum(keep, send):
    return (keep.astype(F32) + swap_cores(send).astype(F32)).astype(BF)


def copies(array):
    return [array] + [lax.ppermute(array, DP, [(i, i ^ k) for i in range(4)]) for k in (1, 2, 3)]


def block(tokens, qkv_weight, pool_kernel, norm_gain, out_weight, out_cotangent):
    shape = tokens.shape
    token_rows = tokens.reshape(HW, WIDTH)
    cotangent_rows = out_cotangent.reshape(HW, WIDTH)
    pool_kernel = jnp.transpose(pool_kernel, (1, 0, 2))
    taps, tap_tokens, part0, part1, part2 = tap_sums(token_rows, qkv_weight, pool_kernel)
    low = to_next(part0)
    up = to_previous(part2)
    qd, *qds = query_side(token_rows, qkv_weight, cotangent_rows, out_weight)
    received = [rotate(q, k) for k, q in zip((1, 2, 3), qds)]
    kv, normed, inv = norm_side(low, part1, up, norm_gain)
    kv = exchange(kv.reshape(32, POS, 2 * SPAN), TM)
    kv = kv.reshape(32 * POS, 2 * SPAN)
    *mds, start = others(received, kv)
    mds = [rotate(m, -k) for k, m in zip((1, 2, 3), mds)]
    md, dkv = own(qd, kv, start)
    parts = exchange(dkv.reshape(32, POS, 2 * SPAN), TM)
    parts = parts.reshape(2, GROUPS, 4, POS, 2 * SPAN)
    d_summed, gain_sum = norm_back(parts, normed, inv, norm_gain)
    d_low = to_next(d_summed)
    d_up = to_previous(d_summed)
    block_out, dq, *pay_a = output_side([md] + mds, token_rows, cotangent_rows, out_weight)
    pay_a = core_sum(*pay_a)
    pay_a = exchange(pay_a, TM)
    pay_a = copies(fold(pay_a))
    dv, send_b, small = pool_back(d_up, d_summed, d_low, taps, tap_tokens, pool_kernel, gain_sum)
    other_small = swap_cores(small)
    other_b = swap_cores(send_b)
    pay_b = pay_b_rows(tap_tokens, dv, other_b, small, other_small)
    pay_b = exchange(pay_b, TM)
    pay_b = copies(fold(pay_b))
    grad_tokens = token_grad(dq, dv, qkv_weight)
    scale = float(HW * lax.axis_size(DP) * lax.axis_size(TM)) ** (-0.5)
    qkv_grad, out_grad, kernel_grad, gain_grad = finish(pay_a, pay_b, scale)
    return (
        block_out.reshape(shape),
        grad_tokens.reshape(shape),
        qkv_grad,
        out_grad,
        jnp.transpose(kernel_grad, (1, 0, 2)),
        gain_grad,
    )


def solution(mesh):
    torus = Mesh(mesh.devices.reshape(2, 2, 2, 4, 4), DP + TM)
    placed = (P(DP, TM, None, None), P(), P(), P(), P(), P(DP, TM, None, None))
    return jax.shard_map(
        block,
        mesh=torus,
        in_specs=placed,
        out_specs=(
            P(DP, TM, None, None),
            P(DP, TM, None, None),
            P(TM, None),
            P(TM, None),
            P(),
            P(),
        ),
        check_vma=False,
    )
```

```python
import jax
import jax.numpy as jnp
from jax import lax
from jax.experimental import pallas as pl
from jax.experimental.pallas import tpu as pltpu
from jax.sharding import Mesh
from jax.sharding import PartitionSpec as P

HEADS = 12
GROUPS = 4
GROUP_HEADS = 3
HEAD = 64
WIDTH = 768
SPAN = GROUP_HEADS * HEAD
HW = 512
TAPS = 288
POS = 32
EPSILON = 1e-05
PAY_B = WIDTH + 256
TM = ("tm_0", "tm_1", "tm_2")
DP = ("dp_0", "dp_1")
BF = jnp.bfloat16
F32 = jnp.float32


def dot(a, b, ca, cb):
    return lax.dot_general(a, b, (((ca,), (cb,)), ((), ())), preferred_element_type=F32)


def params(mib, *semantics):
    return pltpu.CompilerParams(
        dimension_semantics=semantics or None, vmem_limit_bytes=mib * 1024 * 1024
    )


def tap_token(row):
    tap = row >> 5
    i = (row & 31) >> 2
    u = row & 3
    b = jnp.where(tap >= 3, 1, 0) + jnp.where(tap >= 6, 1, 0)
    e = tap - 3 * b
    y = 4 * i + b - 1
    x = 4 * u + e - 1
    return jnp.where((y >= 0) & (x >= 0), y * 16 + x, -1)


def gather_matrix():
    row = lax.broadcasted_iota(jnp.int32, (TAPS, 1), 0)
    token = lax.broadcasted_iota(jnp.int32, (TAPS, HW), 1)
    return jnp.where(token == tap_token(row), 1.0, 0.0).astype(BF)


def scatter_matrix():
    row = lax.broadcasted_iota(jnp.int32, (1, TAPS), 1)
    token = lax.broadcasted_iota(jnp.int32, (HW, TAPS), 0)
    return jnp.where(token == tap_token(row), 1.0, 0.0).astype(BF)


def over_heads(row):
    pair = jnp.concatenate([row, row], axis=-1)
    return jnp.concatenate([pair] * (HEADS // 2), axis=-1)


def head_mean(x):
    rows = x.shape[0]
    chunks = x.shape[1] // 128
    tall = jnp.concatenate([x[:, 128 * k : 128 * k + 128] for k in range(chunks)], axis=0)
    i = lax.broadcasted_iota(jnp.int32, (128, 128), 0) >> 6
    j = lax.broadcasted_iota(jnp.int32, (128, 128), 1) >> 6
    block = jnp.where(i == j, 1.0 / 64.0, 0.0).astype(F32)
    mean = jnp.dot(tall, block, preferred_element_type=F32, precision=lax.Precision.HIGHEST)
    return jnp.concatenate([mean[rows * k : rows * k + rows] for k in range(chunks)], axis=1)


def tap_sums_kernel(tok_ref, w_ref, pk_ref, taps_ref, tt_ref, p0_ref, p1_ref, p2_ref):
    @pl.when(pl.program_id(0) == 0)
    def _():
        tt_ref[...] = dot(gather_matrix(), tok_ref[...], 1, 0).astype(BF)

    taps = dot(tt_ref[...], w_ref[...], 1, 0).astype(BF)
    taps_ref[...] = taps
    wide = taps.astype(F32)
    kernel = over_heads(pk_ref[:, pl.program_id(0), :])
    for a, p_ref in enumerate((p0_ref, p1_ref, p2_ref)):
        total = None
        for be in range(9):
            term = wide[32 * be : 32 * be + 32] * kernel[9 * a + be : 9 * a + be + 1]
            total = term if total is None else total + term
        p_ref[...] = total


def tap_sums(tokens, qkv_weight, pool_kernel):
    part = jax.ShapeDtypeStruct((POS, 2 * WIDTH), F32)
    part_spec = pl.BlockSpec((POS, WIDTH), lambda s: (0, s))
    return pl.pallas_call(
        tap_sums_kernel,
        grid=(2,),
        in_specs=[
            pl.BlockSpec((HW, WIDTH), lambda s: (0, 0)),
            pl.BlockSpec((WIDTH, WIDTH), lambda s: (0, s + 1)),
            pl.BlockSpec((27, 2, HEAD), lambda s: (0, 0, 0)),
        ],
        out_specs=[
            pl.BlockSpec((TAPS, WIDTH), lambda s: (0, s)),
            pl.BlockSpec((TAPS, WIDTH), lambda s: (0, 0)),
            part_spec,
            part_spec,
            part_spec,
        ],
        out_shape=[
            jax.ShapeDtypeStruct((TAPS, 2 * WIDTH), BF),
            jax.ShapeDtypeStruct((TAPS, WIDTH), BF),
            part,
            part,
            part,
        ],
        compiler_params=params(56, "arbitrary"),
        name="tap_sums",
    )(tokens, qkv_weight, pool_kernel)


def query_kernel(tok_ref, w_ref, cot_ref, ow_ref, *refs):
    *out_refs, group_ref = refs
    q = dot(tok_ref[...], w_ref[...], 1, 0).astype(BF)
    dm = dot(cot_ref[...], ow_ref[...], 1, 1).astype(BF)
    for g in range(GROUPS):
        lanes = slice(SPAN * g, SPAN * g + SPAN)
        group_ref[g] = jnp.concatenate([q[:, lanes], dm[:, lanes]], axis=-1)
    mine = lax.axis_index("tm_1")
    for step, out_ref in enumerate(out_refs):
        out_ref[...] = group_ref[(mine + step) % GROUPS]


def query_side(tokens, qkv_weight, cotangent, out_weight):
    full = pl.BlockSpec((HW, WIDTH), lambda i: (0, 0))
    square = pl.BlockSpec((WIDTH, WIDTH), lambda i: (0, 0))
    return pl.pallas_call(
        query_kernel,
        grid=(1,),
        in_specs=[full, square, full, square],
        out_specs=[pl.BlockSpec((HW, 2 * SPAN), lambda i: (0, 0))] * GROUPS,
        out_shape=[jax.ShapeDtypeStruct((HW, 2 * SPAN), BF)] * GROUPS,
        scratch_shapes=[pltpu.VMEM((GROUPS, HW, 2 * SPAN), BF)],
        compiler_params=params(56, "arbitrary"),
        name="query_side",
    )(tokens, qkv_weight, cotangent, out_weight)


def gain_row(gain_ref):
    return jnp.concatenate([over_heads(gain_ref[0:1, :]), over_heads(gain_ref[1:2, :])], axis=-1)


def norm_kernel(low_ref, own_ref, up_ref, gain_ref, kv_ref, normed_ref, inv_ref):
    x = low_ref[...] + own_ref[...] + up_ref[...]
    centred = x - head_mean(x)
    inv = lax.rsqrt(head_mean(centred * centred) + EPSILON)
    normed = centred * inv
    normed_ref[...] = normed
    inv_ref[...] = inv
    pooled = normed * gain_row(gain_ref)
    for g in range(GROUPS):
        k = pooled[:, SPAN * g : SPAN * g + SPAN]
        v = pooled[:, WIDTH + SPAN * g : WIDTH + SPAN * g + SPAN]
        block = jnp.concatenate([k, v], axis=-1).astype(BF)
        for z in range(2):
            for y in range(4):
                kv_ref[z, g, y] = block


def norm_side(low, own, up, gain):
    flat = jax.ShapeDtypeStruct((POS, 2 * WIDTH), F32)
    return pl.pallas_call(
        norm_kernel,
        out_shape=[jax.ShapeDtypeStruct((2, GROUPS, 4, POS, 2 * SPAN), BF), flat, flat],
        compiler_params=params(8),
        name="norm_side",
    )(low, own, up, gain)


def attend(qd, kv_ref, acc_ref):
    n = GROUP_HEADS
    lo = [slice(HEAD * h, HEAD * h + HEAD) for h in range(n)]
    hi = [slice(SPAN + HEAD * h, SPAN + HEAD * h + HEAD) for h in range(n)]
    q = [qd[:, lo[h]] for h in range(n)]
    dm = [qd[:, hi[h]] for h in range(n)]
    k = [kv_ref[:, lo[h]] for h in range(n)]
    v = [kv_ref[:, hi[h]] for h in range(n)]
    s, w, inv, rounded, dp, ds, delta = ({} for _ in range(7))
    mixed, dq = {}, {}
    def score(h):
        s[h] = dot(q[h] * jnp.asarray(0.125, BF), k[h], 1, 1)
    def grad_probs(h):
        dp[h] = dot(dm[h], v[h], 1, 1)
    def soften(h):
        w[h] = jnp.exp(s[h] - jnp.max(s[h], axis=-1, keepdims=True))
        inv[h] = 1.0 / jnp.sum(w[h], axis=-1, keepdims=True)
        rounded[h] = w[h].astype(BF)
    def mix(h):
        attended = lax.transpose(dot(v[h], rounded[h], 0, 1), (1, 0)) * inv[h]
        mixed[h] = (attended + q[h].astype(F32)).astype(BF)
        wide = dm[h].astype(F32)
        delta[h] = jnp.sum(wide * attended, axis=-1, keepdims=True)
    def grad_values(h):
        acc_ref[hi[h], :] += dot((dm[h].astype(F32) * inv[h]).astype(BF), rounded[h], 0, 0)
    def grad_scores(h):
        ds[h] = ((w[h] * inv[h]) * (dp[h] - delta[h])).astype(BF)
    def grad_rest(h):
        dq[h] = (dot(ds[h], k[h], 1, 0) * 0.125 + dm[h].astype(F32)).astype(BF)
        acc_ref[lo[h], :] += dot(q[h], ds[h], 0, 0) * 0.125
    order = (
        (score, 0), (soften, 0), (score, 1), (grad_probs, 0), (mix, 0), (soften, 1),
        (grad_values, 0), (grad_scores, 0), (mix, 1), (grad_probs, 1), (score, 2), (grad_rest, 0),
        (soften, 2), (grad_scores, 1), (grad_values, 1), (mix, 2), (grad_probs, 2), (grad_rest, 1),
        (grad_scores, 2), (grad_values, 2), (grad_rest, 2),
    )
    for function, h in order:
        function(h)
    return jnp.concatenate([mixed[h] for h in range(n)] + [dq[h] for h in range(n)], axis=-1)


def others_kernel(q0_ref, q1_ref, q2_ref, kv_ref, m0_ref, m1_ref, m2_ref, acc_ref, work_ref):
    acc_ref[...] = jnp.zeros_like(acc_ref)
    for n, ref in enumerate((q0_ref, q1_ref, q2_ref)):
        work_ref[n] = ref[...]

    def step(n, carry):
        work_ref[n] = attend(work_ref[n], kv_ref, acc_ref)
        return carry

    lax.fori_loop(0, 3, step, 0)
    for n, ref in enumerate((m0_ref, m1_ref, m2_ref)):
        ref[...] = work_ref[n]


def others(qds, kv):
    block = jax.ShapeDtypeStruct(qds[0].shape, BF)
    return pl.pallas_call(
        others_kernel,
        out_shape=[block, block, block, jax.ShapeDtypeStruct((kv.shape[1], kv.shape[0]), F32)],
        scratch_shapes=[pltpu.VMEM((3,) + block.shape, BF)],
        compiler_params=params(20),
        name="attend_others",
    )(*qds, kv)


def own_kernel(qd_ref, kv_ref, start_ref, md_ref, dkv_ref, acc_ref):
    acc_ref[...] = start_ref[...]
    md_ref[...] = attend(qd_ref[...], kv_ref, acc_ref)
    dkv_ref[...] = jnp.transpose(acc_ref[...]).astype(BF)


def own(qd, kv, start):
    return pl.pallas_call(
        own_kernel,
        out_shape=[jax.ShapeDtypeStruct(qd.shape, BF), jax.ShapeDtypeStruct(kv.shape, BF)],
        scratch_shapes=[pltpu.VMEM(start.shape, F32)],
        compiler_params=params(20),
        name="attend_own",
    )(qd, kv, start)


def norm_back_kernel(parts_ref, normed_ref, inv_ref, gain_ref, d_ref, gsum_ref):
    keys, values = [], []
    for g in range(GROUPS):
        total = None
        for z in range(2):
            for y in range(4):
                term = parts_ref[z, g, y].astype(F32)
                total = term if total is None else total + term
        keys.append(total[:, :SPAN])
        values.append(total[:, SPAN:])
    d_pooled = jnp.concatenate(keys + values, axis=-1)
    normed = normed_ref[...]
    gsum_ref[...] = jnp.sum(d_pooled * normed, axis=0, keepdims=True)
    dn = d_pooled * gain_row(gain_ref)
    d_ref[...] = inv_ref[...] * (dn - head_mean(dn) - normed * head_mean(dn * normed))


def norm_back(parts, normed, inv, gain):
    return pl.pallas_call(
        norm_back_kernel,
        out_shape=[
            jax.ShapeDtypeStruct((POS, 2 * WIDTH), F32),
            jax.ShapeDtypeStruct((1, 2 * WIDTH), F32),
        ],
        compiler_params=params(56),
        name="norm_back",
    )(parts, normed, inv, gain)


def head_sum(x):
    out = []
    for s in range(2):
        pair = x[:, WIDTH * s : WIDTH * s + 128]
        for k in range(1, HEADS // 2):
            pair = pair + x[:, WIDTH * s + 128 * k : WIDTH * s + 128 * k + 128]
        out.append(pair[:, :HEAD] + pair[:, HEAD:])
    return jnp.concatenate(out, axis=-1)


def dest_rows(f):
    return slice(24 * f, 24 * f + 24)


def pool_back_kernel(up_ref, own_ref, low_ref, taps_ref, tt_ref, pk_ref, gsum_ref, *out_refs):
    dv_ref, send_ref, small_ref = out_refs
    sources = (up_ref[...], own_ref[...], low_ref[...])
    for s in range(2):
        lanes = slice(WIDTH * s, WIDTH * s + WIDTH)
        kernel = over_heads(pk_ref[:, s, :])
        for be in range(9):
            total = None
            for a in range(3):
                term = sources[a][:, lanes] * kernel[9 * a + be : 9 * a + be + 1]
                total = term if total is None else total + term
            dv_ref[s, 32 * be : 32 * be + 32, :] = total.astype(BF)
    grads = dot(tt_ref[...], dv_ref[1 - lax.axis_index("dp_1")], 0, 0)
    for f in range(32):
        send_ref[f] = grads[dest_rows(f)].astype(BF)
    tap_rows = []
    for a in range(3):
        for be in range(9):
            tap = taps_ref[32 * be : 32 * be + 32, :].astype(F32)
            tap_rows.append(jnp.sum(sources[a] * tap, axis=0, keepdims=True))
    small = head_sum(jnp.concatenate(tap_rows + [gsum_ref[...]], axis=0))
    second = jnp.concatenate([small[24:28], jnp.zeros((20, 128), F32)], axis=0)
    small_ref[...] = jnp.concatenate([small[0:24], second], axis=-1)


def pool_back(up, own, low, taps, tap_tokens, pool_kernel, gain_sum):
    return pl.pallas_call(
        pool_back_kernel,
        out_shape=[
            jax.ShapeDtypeStruct((2, TAPS, WIDTH), BF),
            jax.ShapeDtypeStruct((32, 24, WIDTH), BF),
            jax.ShapeDtypeStruct((24, 256), F32),
        ],
        compiler_params=params(56),
        name="pool_back",
    )(up, own, low, taps, tap_tokens, pool_kernel, gain_sum)


def pay_b_kernel(tt_ref, dv_ref, other_ref, small_ref, other_small_ref, out_ref):
    core = lax.axis_index("dp_1")
    grads = dot(tt_ref[...], dv_ref[core], 0, 0)
    small = small_ref[...] + other_small_ref[...]
    high = small.astype(BF).astype(F32)
    extra = jnp.where(core == 0, high, small - high).astype(BF)
    for f in range(32):
        total = grads[dest_rows(f)] + other_ref[f].astype(F32)
        out_ref[f, :, :WIDTH] = total.astype(BF)
        out_ref[f, :, WIDTH:] = extra


def pay_b_rows(tap_tokens, dv, other, small, other_small):
    return pl.pallas_call(
        pay_b_kernel,
        out_shape=jax.ShapeDtypeStruct((32, 24, PAY_B), BF),
        compiler_params=params(16),
        name="pay_b_rows",
    )(tap_tokens, dv, other, small, other_small)


def output_kernel(m0_ref, m1_ref, m2_ref, m3_ref, tok_ref, cot_ref, ow_ref, *refs):
    out_ref, dq_ref, keep_ref, send_ref, group_ref, half_ref = refs
    mine = lax.axis_index("tm_1")
    for step, ref in enumerate((m0_ref, m1_ref, m2_ref, m3_ref)):
        group_ref[(mine + step) % GROUPS] = ref[...]
    mixed = jnp.concatenate([group_ref[g, :, :SPAN] for g in range(GROUPS)], axis=-1)
    dq = jnp.concatenate([group_ref[g, :, SPAN:] for g in range(GROUPS)], axis=-1)
    dq_ref[...] = dq
    out_ref[...] = dot(mixed, ow_ref[...], 1, 0).astype(BF)
    q_grad = dot(tok_ref[...], dq, 0, 0)
    o_grad = dot(mixed, cot_ref[...], 0, 0)
    for f in range(32):
        rows = slice(24 * f, 24 * f + 24)
        half_ref[0, f] = q_grad[rows].astype(BF)
        half_ref[1, f] = o_grad[rows].astype(BF)
    core = lax.axis_index("dp_1")
    keep_ref[...] = half_ref[core]
    send_ref[...] = half_ref[1 - core]


def output_side(mds, tokens, cotangent, out_weight):
    half = jax.ShapeDtypeStruct((32, 24, WIDTH), BF)
    rows = jax.ShapeDtypeStruct((HW, WIDTH), BF)
    return pl.pallas_call(
        output_kernel,
        out_shape=[rows, rows, half, half],
        scratch_shapes=[
            pltpu.VMEM((GROUPS, HW, 2 * SPAN), BF),
            pltpu.VMEM((2, 32, 24, WIDTH), BF),
        ],
        compiler_params=params(56),
        name="output_side",
    )(*mds, tokens, cotangent, out_weight)


def token_grad_kernel(dq_ref, dv_ref, w_ref, out_ref):
    scatter = scatter_matrix()
    total = dot(dq_ref[...], w_ref[:, :WIDTH], 1, 1)
    for s in range(2):
        spread = dot(scatter, dv_ref[s], 1, 0).astype(BF)
        total += dot(spread, w_ref[:, WIDTH * (s + 1) : WIDTH * (s + 2)], 1, 1)
    out_ref[...] = total.astype(BF)


def token_grad(dq, dv, qkv_weight):
    return pl.pallas_call(
        token_grad_kernel,
        out_shape=jax.ShapeDtypeStruct((HW, WIDTH), BF),
        compiler_params=params(56),
        name="token_grad",
    )(dq, dv, qkv_weight)


def fold_kernel(parts_ref, out_ref):
    total = parts_ref[0].astype(F32)
    for f in range(1, 32):
        total = total + parts_ref[f].astype(F32)
    out_ref[...] = total


def fold(parts):
    return pl.pallas_call(
        fold_kernel,
        out_shape=jax.ShapeDtypeStruct(parts.shape[1:], F32),
        compiler_params=params(8),
        name="fold",
    )(parts)


def finish_kernel(scale, a0, a1, a2, a3, b0, b1, b2, b3, qkv_ref, out_ref, kernel_ref, gain_ref, a_ref, b_ref):
    core = lax.axis_index("dp_1")
    a_ref[core] = (a0[...] + a2[...]) * scale
    a_ref[1 - core] = (a1[...] + a3[...]) * scale
    b_ref[core] = (b0[...] + b2[...]) * scale
    b_ref[1 - core] = (b1[...] + b3[...]) * scale
    qkv_ref[:, :WIDTH] = a_ref[0]
    qkv_ref[:, WIDTH : 2 * WIDTH] = b_ref[0, :, :WIDTH]
    qkv_ref[:, 2 * WIDTH :] = b_ref[1, :, :WIDTH]
    out_ref[...] = a_ref[1]
    small = b_ref[0, :, WIDTH:] + b_ref[1, :, WIDTH:]
    first = small[:, :128]
    second = small[:, 128:]
    for s in range(2):
        lanes = slice(HEAD * s, HEAD * s + HEAD)
        kernel_ref[0:24, s, :] = first[:, lanes]
        kernel_ref[24:27, s, :] = second[0:3, lanes]
        gain_ref[s : s + 1, :] = second[3:4, lanes]


def finish(a, b, scale):
    return pl.pallas_call(
        lambda *refs: finish_kernel(scale, *refs),
        out_shape=[
            jax.ShapeDtypeStruct((24, 3 * WIDTH), F32),
            jax.ShapeDtypeStruct((24, WIDTH), F32),
            jax.ShapeDtypeStruct((27, 2, HEAD), F32),
            jax.ShapeDtypeStruct((2, HEAD), F32),
        ],
        scratch_shapes=[pltpu.VMEM((2, 24, WIDTH), F32), pltpu.VMEM((2, 24, PAY_B), F32)],
        compiler_params=params(56),
        name="finish",
    )(*a, *b)


def exchange(array, axis):
    return lax.all_to_all(array, axis, split_axis=0, concat_axis=0, tiled=True)


def to_next(array):
    return lax.ppermute(array, TM, [(i, i + 1) for i in range(lax.axis_size(TM) - 1)])


def to_previous(array):
    return lax.ppermute(array, TM, [(i + 1, i) for i in range(lax.axis_size(TM) - 1)])


def rotate(array, steps):
    return lax.ppermute(array, "tm_1", [(i, (i + steps) % GROUPS) for i in range(GROUPS)])


def swap_cores(array):
    return lax.ppermute(array, "dp_1", [(0, 1), (1, 0)])


def core_sum(keep, send):
    return (keep.astype(F32) + swap_cores(send).astype(F32)).astype(BF)


def copies(array):
    return [array] + [lax.ppermute(array, DP, [(i, i ^ k) for i in range(4)]) for k in (1, 2, 3)]


def block(tokens, qkv_weight, pool_kernel, norm_gain, out_weight, out_cotangent):
    shape = tokens.shape
    token_rows = tokens.reshape(HW, WIDTH)
    cotangent_rows = out_cotangent.reshape(HW, WIDTH)
    pool_kernel = jnp.transpose(pool_kernel, (1, 0, 2))
    taps, tap_tokens, part0, part1, part2 = tap_sums(token_rows, qkv_weight, pool_kernel)
    low = to_next(part0)
    up = to_previous(part2)
    qd, *qds = query_side(token_rows, qkv_weight, cotangent_rows, out_weight)
    received = [rotate(q, k) for k, q in zip((1, 2, 3), qds)]
    kv, normed, inv = norm_side(low, part1, up, norm_gain)
    kv = exchange(kv.reshape(32, POS, 2 * SPAN), TM)
    kv = kv.reshape(32 * POS, 2 * SPAN)
    *mds, start = others(received, kv)
    mds = [rotate(m, -k) for k, m in zip((1, 2, 3), mds)]
    md, dkv = own(qd, kv, start)
    parts = exchange(dkv.reshape(32, POS, 2 * SPAN), TM)
    parts = parts.reshape(2, GROUPS, 4, POS, 2 * SPAN)
    d_summed, gain_sum = norm_back(parts, normed, inv, norm_gain)
    d_low = to_next(d_summed)
    d_up = to_previous(d_summed)
    block_out, dq, *pay_a = output_side([md] + mds, token_rows, cotangent_rows, out_weight)
    pay_a = core_sum(*pay_a)
    pay_a = exchange(pay_a, TM)
    pay_a = copies(fold(pay_a))
    dv, send_b, small = pool_back(d_up, d_summed, d_low, taps, tap_tokens, pool_kernel, gain_sum)
    other_small = swap_cores(small)
    other_b = swap_cores(send_b)
    pay_b = pay_b_rows(tap_tokens, dv, other_b, small, other_small)
    pay_b = exchange(pay_b, TM)
    pay_b = copies(fold(pay_b))
    grad_tokens = token_grad(dq, dv, qkv_weight)
    scale = float(HW * lax.axis_size(DP) * lax.axis_size(TM)) ** (-0.5)
    qkv_grad, out_grad, kernel_grad, gain_grad = finish(pay_a, pay_b, scale)
    return (
        block_out.reshape(shape),
        grad_tokens.reshape(shape),
        qkv_grad,
        out_grad,
        jnp.transpose(kernel_grad, (1, 0, 2)),
        gain_grad,
    )


def solution(mesh):
    torus = Mesh(mesh.devices.reshape(2, 2, 2, 4, 4), DP + TM)
    placed = (P(DP, TM, None, None), P(), P(), P(), P(), P(DP, TM, None, None))
    return jax.shard_map(
        block,
        mesh=torus,
        in_specs=placed,
        out_specs=(
            P(DP, TM, None, None),
            P(DP, TM, None, None),
            P(TM, None),
            P(TM, None),
            P(),
            P(),
        ),
        check_vma=False,
    )
```

```python
import jax
import jax.numpy as jnp
from jax import lax
from jax.experimental import pallas as pl
from jax.experimental.pallas import tpu as pltpu
from jax.sharding import Mesh
from jax.sharding import PartitionSpec as P

HEADS = 12
GROUPS = 4
GROUP_HEADS = 3
HEAD = 64
WIDTH = 768
SPAN = GROUP_HEADS * HEAD
HW = 512
TAPS = 288
POS = 32
EPSILON = 1e-05
PAY_B = WIDTH + 256
TM = ("tm_0", "tm_1", "tm_2")
DP = ("dp_0", "dp_1")
BF = jnp.bfloat16
F32 = jnp.float32


def dot(a, b, ca, cb):
    return lax.dot_general(a, b, (((ca,), (cb,)), ((), ())), preferred_element_type=F32)


def params(mib, *semantics):
    return pltpu.CompilerParams(
        dimension_semantics=semantics or None, vmem_limit_bytes=mib * 1024 * 1024
    )


def tap_token(row):
    tap = row >> 5
    i = (row & 31) >> 2
    u = row & 3
    b = jnp.where(tap >= 3, 1, 0) + jnp.where(tap >= 6, 1, 0)
    e = tap - 3 * b
    y = 4 * i + b - 1
    x = 4 * u + e - 1
    return jnp.where((y >= 0) & (x >= 0), y * 16 + x, -1)


def gather_matrix():
    row = lax.broadcasted_iota(jnp.int32, (TAPS, 1), 0)
    token = lax.broadcasted_iota(jnp.int32, (TAPS, HW), 1)
    return jnp.where(token == tap_token(row), 1.0, 0.0).astype(BF)


def scatter_matrix():
    row = lax.broadcasted_iota(jnp.int32, (1, TAPS), 1)
    token = lax.broadcasted_iota(jnp.int32, (HW, TAPS), 0)
    return jnp.where(token == tap_token(row), 1.0, 0.0).astype(BF)


def over_heads(row):
    pair = jnp.concatenate([row, row], axis=-1)
    return jnp.concatenate([pair] * (HEADS // 2), axis=-1)


def head_mean(x):
    rows = x.shape[0]
    chunks = x.shape[1] // 128
    tall = jnp.concatenate([x[:, 128 * k : 128 * k + 128] for k in range(chunks)], axis=0)
    i = lax.broadcasted_iota(jnp.int32, (128, 128), 0) >> 6
    j = lax.broadcasted_iota(jnp.int32, (128, 128), 1) >> 6
    block = jnp.where(i == j, 1.0 / 64.0, 0.0).astype(F32)
    mean = jnp.dot(tall, block, preferred_element_type=F32, precision=lax.Precision.HIGHEST)
    return jnp.concatenate([mean[rows * k : rows * k + rows] for k in range(chunks)], axis=1)


def tap_sums_kernel(tok_ref, w_ref, pk_ref, taps_ref, tt_ref, p0_ref, p1_ref, p2_ref):
    @pl.when(pl.program_id(0) == 0)
    def _():
        tt_ref[...] = dot(gather_matrix(), tok_ref[...], 1, 0).astype(BF)

    taps = dot(tt_ref[...], w_ref[...], 1, 0).astype(BF)
    taps_ref[...] = taps
    wide = taps.astype(F32)
    kernel = over_heads(pk_ref[:, pl.program_id(0), :])
    for a, p_ref in enumerate((p0_ref, p1_ref, p2_ref)):
        total = None
        for be in range(9):
            term = wide[32 * be : 32 * be + 32] * kernel[9 * a + be : 9 * a + be + 1]
            total = term if total is None else total + term
        p_ref[...] = total


def tap_sums(tokens, qkv_weight, pool_kernel):
    part = jax.ShapeDtypeStruct((POS, 2 * WIDTH), F32)
    part_spec = pl.BlockSpec((POS, WIDTH), lambda s: (0, s))
    return pl.pallas_call(
        tap_sums_kernel,
        grid=(2,),
        in_specs=[
            pl.BlockSpec((HW, WIDTH), lambda s: (0, 0)),
            pl.BlockSpec((WIDTH, WIDTH), lambda s: (0, s + 1)),
            pl.BlockSpec((27, 2, HEAD), lambda s: (0, 0, 0)),
        ],
        out_specs=[
            pl.BlockSpec((TAPS, WIDTH), lambda s: (0, s)),
            pl.BlockSpec((TAPS, WIDTH), lambda s: (0, 0)),
            part_spec,
            part_spec,
            part_spec,
        ],
        out_shape=[
            jax.ShapeDtypeStruct((TAPS, 2 * WIDTH), BF),
            jax.ShapeDtypeStruct((TAPS, WIDTH), BF),
            part,
            part,
            part,
        ],
        compiler_params=params(56, "arbitrary"),
        name="tap_sums",
    )(tokens, qkv_weight, pool_kernel)


def query_kernel(tok_ref, w_ref, cot_ref, ow_ref, *refs):
    *out_refs, group_ref = refs
    q = dot(tok_ref[...], w_ref[...], 1, 0).astype(BF)
    dm = dot(cot_ref[...], ow_ref[...], 1, 1).astype(BF)
    for g in range(GROUPS):
        lanes = slice(SPAN * g, SPAN * g + SPAN)
        group_ref[g] = jnp.concatenate([q[:, lanes], dm[:, lanes]], axis=-1)
    mine = lax.axis_index("tm_1")
    for step, out_ref in enumerate(out_refs):
        out_ref[...] = group_ref[(mine + step) % GROUPS]


def query_side(tokens, qkv_weight, cotangent, out_weight):
    full = pl.BlockSpec((HW, WIDTH), lambda i: (0, 0))
    square = pl.BlockSpec((WIDTH, WIDTH), lambda i: (0, 0))
    return pl.pallas_call(
        query_kernel,
        grid=(1,),
        in_specs=[full, square, full, square],
        out_specs=[pl.BlockSpec((HW, 2 * SPAN), lambda i: (0, 0))] * GROUPS,
        out_shape=[jax.ShapeDtypeStruct((HW, 2 * SPAN), BF)] * GROUPS,
        scratch_shapes=[pltpu.VMEM((GROUPS, HW, 2 * SPAN), BF)],
        compiler_params=params(56, "arbitrary"),
        name="query_side",
    )(tokens, qkv_weight, cotangent, out_weight)


def gain_row(gain_ref):
    return jnp.concatenate([over_heads(gain_ref[0:1, :]), over_heads(gain_ref[1:2, :])], axis=-1)


def norm_kernel(low_ref, own_ref, up_ref, gain_ref, kv_ref, normed_ref, inv_ref):
    x = low_ref[...] + own_ref[...] + up_ref[...]
    centred = x - head_mean(x)
    inv = lax.rsqrt(head_mean(centred * centred) + EPSILON)
    normed = centred * inv
    normed_ref[...] = normed
    inv_ref[...] = inv
    pooled = normed * gain_row(gain_ref)
    for g in range(GROUPS):
        k = pooled[:, SPAN * g : SPAN * g + SPAN]
        v = pooled[:, WIDTH + SPAN * g : WIDTH + SPAN * g + SPAN]
        block = jnp.concatenate([k, v], axis=-1).astype(BF)
        for z in range(2):
            for y in range(4):
                kv_ref[z, g, y] = block


def norm_side(low, own, up, gain):
    flat = jax.ShapeDtypeStruct((POS, 2 * WIDTH), F32)
    return pl.pallas_call(
        norm_kernel,
        out_shape=[jax.ShapeDtypeStruct((2, GROUPS, 4, POS, 2 * SPAN), BF), flat, flat],
        compiler_params=params(8),
        name="norm_side",
    )(low, own, up, gain)


def attend(qd, kv_ref, acc_ref):
    n = GROUP_HEADS
    lo = [slice(HEAD * h, HEAD * h + HEAD) for h in range(n)]
    hi = [slice(SPAN + HEAD * h, SPAN + HEAD * h + HEAD) for h in range(n)]
    q = [qd[:, lo[h]] for h in range(n)]
    dm = [qd[:, hi[h]] for h in range(n)]
    k = [kv_ref[:, lo[h]] for h in range(n)]
    v = [kv_ref[:, hi[h]] for h in range(n)]
    s, w, inv, rounded, dp, ds, delta = ({} for _ in range(7))
    mixed, dq = {}, {}
    def score(h):
        s[h] = dot(q[h] * jnp.asarray(0.125, BF), k[h], 1, 1)
    def grad_probs(h):
        dp[h] = dot(dm[h], v[h], 1, 1)
    def soften(h):
        w[h] = jnp.exp(s[h] - jnp.max(s[h], axis=-1, keepdims=True))
        inv[h] = 1.0 / jnp.sum(w[h], axis=-1, keepdims=True)
        rounded[h] = w[h].astype(BF)
    def mix(h):
        attended = lax.transpose(dot(v[h], rounded[h], 0, 1), (1, 0)) * inv[h]
        mixed[h] = (attended + q[h].astype(F32)).astype(BF)
        wide = dm[h].astype(F32)
        delta[h] = jnp.sum(wide * attended, axis=-1, keepdims=True)
    def grad_values(h):
        acc_ref[hi[h], :] += dot((dm[h].astype(F32) * inv[h]).astype(BF), rounded[h], 0, 0)
    def grad_scores(h):
        ds[h] = ((w[h] * inv[h]) * (dp[h] - delta[h])).astype(BF)
    def grad_rest(h):
        dq[h] = (dot(ds[h], k[h], 1, 0) * 0.125 + dm[h].astype(F32)).astype(BF)
        acc_ref[lo[h], :] += dot(q[h], ds[h], 0, 0) * 0.125
    order = (
        (score, 0), (soften, 0), (score, 1), (grad_probs, 0), (mix, 0), (soften, 1),
        (grad_values, 0), (grad_scores, 0), (mix, 1), (grad_probs, 1), (score, 2), (grad_rest, 0),
        (soften, 2), (grad_scores, 1), (grad_values, 1), (mix, 2), (grad_probs, 2), (grad_rest, 1),
        (grad_scores, 2), (grad_values, 2), (grad_rest, 2),
    )
    for function, h in order:
        function(h)
    return jnp.concatenate([mixed[h] for h in range(n)] + [dq[h] for h in range(n)], axis=-1)


def others_kernel(q0_ref, q1_ref, q2_ref, kv_ref, m0_ref, m1_ref, m2_ref, acc_ref, work_ref):
    acc_ref[...] = jnp.zeros_like(acc_ref)
    for n, ref in enumerate((q0_ref, q1_ref, q2_ref)):
        work_ref[n] = ref[...]

    def step(n, carry):
        work_ref[n] = attend(work_ref[n], kv_ref, acc_ref)
        return carry

    lax.fori_loop(0, 3, step, 0)
    for n, ref in enumerate((m0_ref, m1_ref, m2_ref)):
        ref[...] = work_ref[n]


def others(qds, kv):
    block = jax.ShapeDtypeStruct(qds[0].shape, BF)
    return pl.pallas_call(
        others_kernel,
        out_shape=[block, block, block, jax.ShapeDtypeStruct((kv.shape[1], kv.shape[0]), F32)],
        scratch_shapes=[pltpu.VMEM((3,) + block.shape, BF)],
        compiler_params=params(20),
        name="attend_others",
    )(*qds, kv)


def own_kernel(qd_ref, kv_ref, start_ref, md_ref, dkv_ref, acc_ref):
    acc_ref[...] = start_ref[...]
    md_ref[...] = attend(qd_ref[...], kv_ref, acc_ref)
    dkv_ref[...] = jnp.transpose(acc_ref[...]).astype(BF)


def own(qd, kv, start):
    return pl.pallas_call(
        own_kernel,
        out_shape=[jax.ShapeDtypeStruct(qd.shape, BF), jax.ShapeDtypeStruct(kv.shape, BF)],
        scratch_shapes=[pltpu.VMEM(start.shape, F32)],
        compiler_params=params(20),
        name="attend_own",
    )(qd, kv, start)


def norm_back_kernel(parts_ref, normed_ref, inv_ref, gain_ref, d_ref, gsum_ref):
    keys, values = [], []
    for g in range(GROUPS):
        total = None
        for z in range(2):
            for y in range(4):
                term = parts_ref[z, g, y].astype(F32)
                total = term if total is None else total + term
        keys.append(total[:, :SPAN])
        values.append(total[:, SPAN:])
    d_pooled = jnp.concatenate(keys + values, axis=-1)
    normed = normed_ref[...]
    gsum_ref[...] = jnp.sum(d_pooled * normed, axis=0, keepdims=True)
    dn = d_pooled * gain_row(gain_ref)
    d_ref[...] = inv_ref[...] * (dn - head_mean(dn) - normed * head_mean(dn * normed))


def norm_back(parts, normed, inv, gain):
    return pl.pallas_call(
        norm_back_kernel,
        out_shape=[
            jax.ShapeDtypeStruct((POS, 2 * WIDTH), F32),
            jax.ShapeDtypeStruct((1, 2 * WIDTH), F32),
        ],
        compiler_params=params(40),
        name="norm_back",
    )(parts, normed, inv, gain)


def head_sum(x):
    out = []
    for s in range(2):
        pair = x[:, WIDTH * s : WIDTH * s + 128]
        for k in range(1, HEADS // 2):
            pair = pair + x[:, WIDTH * s + 128 * k : WIDTH * s + 128 * k + 128]
        out.append(pair[:, :HEAD] + pair[:, HEAD:])
    return jnp.concatenate(out, axis=-1)


def dest_rows(f):
    return slice(24 * f, 24 * f + 24)


def pool_back_kernel(up_ref, own_ref, low_ref, taps_ref, tt_ref, pk_ref, gsum_ref, *out_refs):
    dv_ref, send_ref, small_ref = out_refs
    sources = (up_ref[...], own_ref[...], low_ref[...])
    for s in range(2):
        lanes = slice(WIDTH * s, WIDTH * s + WIDTH)
        kernel = over_heads(pk_ref[:, s, :])
        for be in range(9):
            total = None
            for a in range(3):
                term = sources[a][:, lanes] * kernel[9 * a + be : 9 * a + be + 1]
                total = term if total is None else total + term
            dv_ref[s, 32 * be : 32 * be + 32, :] = total.astype(BF)
    grads = dot(tt_ref[...], dv_ref[1 - lax.axis_index("dp_1")], 0, 0)
    for f in range(32):
        send_ref[f] = grads[dest_rows(f)].astype(BF)
    tap_rows = []
    for a in range(3):
        for be in range(9):
            tap = taps_ref[32 * be : 32 * be + 32, :].astype(F32)
            tap_rows.append(jnp.sum(sources[a] * tap, axis=0, keepdims=True))
    small = head_sum(jnp.concatenate(tap_rows + [gsum_ref[...]], axis=0))
    second = jnp.concatenate([small[24:28], jnp.zeros((20, 128), F32)], axis=0)
    small_ref[...] = jnp.concatenate([small[0:24], second], axis=-1)


def pool_back(up, own, low, taps, tap_tokens, pool_kernel, gain_sum):
    return pl.pallas_call(
        pool_back_kernel,
        out_shape=[
            jax.ShapeDtypeStruct((2, TAPS, WIDTH), BF),
            jax.ShapeDtypeStruct((32, 24, WIDTH), BF),
            jax.ShapeDtypeStruct((24, 256), F32),
        ],
        compiler_params=params(40),
        name="pool_back",
    )(up, own, low, taps, tap_tokens, pool_kernel, gain_sum)


def pay_b_kernel(tt_ref, dv_ref, other_ref, small_ref, other_small_ref, out_ref):
    core = lax.axis_index("dp_1")
    grads = dot(tt_ref[...], dv_ref[core], 0, 0)
    small = small_ref[...] + other_small_ref[...]
    high = small.astype(BF).astype(F32)
    extra = jnp.where(core == 0, high, small - high).astype(BF)
    for f in range(32):
        total = grads[dest_rows(f)] + other_ref[f].astype(F32)
        out_ref[f, :, :WIDTH] = total.astype(BF)
        out_ref[f, :, WIDTH:] = extra


def pay_b_rows(tap_tokens, dv, other, small, other_small):
    return pl.pallas_call(
        pay_b_kernel,
        out_shape=jax.ShapeDtypeStruct((32, 24, PAY_B), BF),
        compiler_params=params(16),
        name="pay_b_rows",
    )(tap_tokens, dv, other, small, other_small)


def output_kernel(m0_ref, m1_ref, m2_ref, m3_ref, tok_ref, cot_ref, ow_ref, *refs):
    out_ref, dq_ref, keep_ref, send_ref, group_ref, half_ref = refs
    mine = lax.axis_index("tm_1")
    for step, ref in enumerate((m0_ref, m1_ref, m2_ref, m3_ref)):
        group_ref[(mine + step) % GROUPS] = ref[...]
    mixed = jnp.concatenate([group_ref[g, :, :SPAN] for g in range(GROUPS)], axis=-1)
    dq = jnp.concatenate([group_ref[g, :, SPAN:] for g in range(GROUPS)], axis=-1)
    dq_ref[...] = dq
    out_ref[...] = dot(mixed, ow_ref[...], 1, 0).astype(BF)
    q_grad = dot(tok_ref[...], dq, 0, 0)
    o_grad = dot(mixed, cot_ref[...], 0, 0)
    for f in range(32):
        rows = slice(24 * f, 24 * f + 24)
        half_ref[0, f] = q_grad[rows].astype(BF)
        half_ref[1, f] = o_grad[rows].astype(BF)
    core = lax.axis_index("dp_1")
    keep_ref[...] = half_ref[core]
    send_ref[...] = half_ref[1 - core]


def output_side(mds, tokens, cotangent, out_weight):
    half = jax.ShapeDtypeStruct((32, 24, WIDTH), BF)
    rows = jax.ShapeDtypeStruct((HW, WIDTH), BF)
    return pl.pallas_call(
        output_kernel,
        out_shape=[rows, rows, half, half],
        scratch_shapes=[
            pltpu.VMEM((GROUPS, HW, 2 * SPAN), BF),
            pltpu.VMEM((2, 32, 24, WIDTH), BF),
        ],
        compiler_params=params(56),
        name="output_side",
    )(*mds, tokens, cotangent, out_weight)


def token_grad_kernel(dq_ref, dv_ref, w_ref, out_ref):
    scatter = scatter_matrix()
    total = dot(dq_ref[...], w_ref[:, :WIDTH], 1, 1)
    for s in range(2):
        spread = dot(scatter, dv_ref[s], 1, 0).astype(BF)
        total += dot(spread, w_ref[:, WIDTH * (s + 1) : WIDTH * (s + 2)], 1, 1)
    out_ref[...] = total.astype(BF)


def token_grad(dq, dv, qkv_weight):
    return pl.pallas_call(
        token_grad_kernel,
        out_shape=jax.ShapeDtypeStruct((HW, WIDTH), BF),
        compiler_params=params(56),
        name="token_grad",
    )(dq, dv, qkv_weight)


def fold_kernel(parts_ref, out_ref):
    total = parts_ref[0].astype(F32)
    for f in range(1, 32):
        total = total + parts_ref[f].astype(F32)
    out_ref[...] = total


def fold(parts):
    return pl.pallas_call(
        fold_kernel,
        out_shape=jax.ShapeDtypeStruct(parts.shape[1:], F32),
        compiler_params=params(8),
        name="fold",
    )(parts)


def finish_kernel(scale, a0, a1, a2, a3, b0, b1, b2, b3, qkv_ref, out_ref, kernel_ref, gain_ref, a_ref, b_ref):
    core = lax.axis_index("dp_1")
    a_ref[core] = (a0[...] + a2[...]) * scale
    a_ref[1 - core] = (a1[...] + a3[...]) * scale
    b_ref[core] = (b0[...] + b2[...]) * scale
    b_ref[1 - core] = (b1[...] + b3[...]) * scale
    qkv_ref[:, :WIDTH] = a_ref[0]
    qkv_ref[:, WIDTH : 2 * WIDTH] = b_ref[0, :, :WIDTH]
    qkv_ref[:, 2 * WIDTH :] = b_ref[1, :, :WIDTH]
    out_ref[...] = a_ref[1]
    small = b_ref[0, :, WIDTH:] + b_ref[1, :, WIDTH:]
    first = small[:, :128]
    second = small[:, 128:]
    for s in range(2):
        lanes = slice(HEAD * s, HEAD * s + HEAD)
        kernel_ref[0:24, s, :] = first[:, lanes]
        kernel_ref[24:27, s, :] = second[0:3, lanes]
        gain_ref[s : s + 1, :] = second[3:4, lanes]


def finish(a, b, scale):
    return pl.pallas_call(
        lambda *refs: finish_kernel(scale, *refs),
        out_shape=[
            jax.ShapeDtypeStruct((24, 3 * WIDTH), F32),
            jax.ShapeDtypeStruct((24, WIDTH), F32),
            jax.ShapeDtypeStruct((27, 2, HEAD), F32),
            jax.ShapeDtypeStruct((2, HEAD), F32),
        ],
        scratch_shapes=[pltpu.VMEM((2, 24, WIDTH), F32), pltpu.VMEM((2, 24, PAY_B), F32)],
        compiler_params=params(8),
        name="finish",
    )(*a, *b)


def exchange(array, axis):
    return lax.all_to_all(array, axis, split_axis=0, concat_axis=0, tiled=True)


def to_next(array):
    return lax.ppermute(array, TM, [(i, i + 1) for i in range(lax.axis_size(TM) - 1)])


def to_previous(array):
    return lax.ppermute(array, TM, [(i + 1, i) for i in range(lax.axis_size(TM) - 1)])


def rotate(array, steps):
    return lax.ppermute(array, "tm_1", [(i, (i + steps) % GROUPS) for i in range(GROUPS)])


def swap_cores(array):
    return lax.ppermute(array, "dp_1", [(0, 1), (1, 0)])


def core_sum(keep, send):
    return (keep.astype(F32) + swap_cores(send).astype(F32)).astype(BF)


def copies(array):
    return [array] + [lax.ppermute(array, DP, [(i, i ^ k) for i in range(4)]) for k in (1, 2, 3)]


def block(tokens, qkv_weight, pool_kernel, norm_gain, out_weight, out_cotangent):
    shape = tokens.shape
    token_rows = tokens.reshape(HW, WIDTH)
    cotangent_rows = out_cotangent.reshape(HW, WIDTH)
    pool_kernel = jnp.transpose(pool_kernel, (1, 0, 2))
    taps, tap_tokens, part0, part1, part2 = tap_sums(token_rows, qkv_weight, pool_kernel)
    low = to_next(part0)
    up = to_previous(part2)
    qd, *qds = query_side(token_rows, qkv_weight, cotangent_rows, out_weight)
    received = [rotate(q, k) for k, q in zip((1, 2, 3), qds)]
    kv, normed, inv = norm_side(low, part1, up, norm_gain)
    kv = exchange(kv.reshape(32, POS, 2 * SPAN), TM)
    kv = kv.reshape(32 * POS, 2 * SPAN)
    *mds, start = others(received, kv)
    mds = [rotate(m, -k) for k, m in zip((1, 2, 3), mds)]
    md, dkv = own(qd, kv, start)
    parts = exchange(dkv.reshape(32, POS, 2 * SPAN), TM)
    parts = parts.reshape(2, GROUPS, 4, POS, 2 * SPAN)
    d_summed, gain_sum = norm_back(parts, normed, inv, norm_gain)
    d_low = to_next(d_summed)
    d_up = to_previous(d_summed)
    block_out, dq, *pay_a = output_side([md] + mds, token_rows, cotangent_rows, out_weight)
    pay_a = core_sum(*pay_a)
    pay_a = exchange(pay_a, TM)
    pay_a = copies(fold(pay_a))
    dv, send_b, small = pool_back(d_up, d_summed, d_low, taps, tap_tokens, pool_kernel, gain_sum)
    other_small = swap_cores(small)
    other_b = swap_cores(send_b)
    pay_b = pay_b_rows(tap_tokens, dv, other_b, small, other_small)
    pay_b = exchange(pay_b, TM)
    pay_b = copies(fold(pay_b))
    grad_tokens = token_grad(dq, dv, qkv_weight)
    scale = float(HW * lax.axis_size(DP) * lax.axis_size(TM)) ** (-0.5)
    qkv_grad, out_grad, kernel_grad, gain_grad = finish(pay_a, pay_b, scale)
    return (
        block_out.reshape(shape),
        grad_tokens.reshape(shape),
        qkv_grad,
        out_grad,
        jnp.transpose(kernel_grad, (1, 0, 2)),
        gain_grad,
    )


def solution(mesh):
    torus = Mesh(mesh.devices.reshape(2, 2, 2, 4, 4), DP + TM)
    placed = (P(DP, TM, None, None), P(), P(), P(), P(), P(DP, TM, None, None))
    return jax.shard_map(
        block,
        mesh=torus,
        in_specs=placed,
        out_specs=(
            P(DP, TM, None, None),
            P(DP, TM, None, None),
            P(TM, None),
            P(TM, None),
            P(),
            P(),
        ),
        check_vma=False,
    )
```
